32 devices in a mesh: dp: 2 (over core), fsdp: 16 (over z, y, x).
Axes of the slice: x: 2, y: 2, z: 4, core: 2. Of those that a mesh axis runs over, the one named last changes fastest.
Arguments:
- tokens: bfloat16 [38080, 768], P(('dp', 'fsdp')), may hold values from -6 to 6
- cotangent: bfloat16 [38080, 768], P(('dp', 'fsdp')), may hold values from -6 to 6
- segments: int32 [38080], P(('dp', 'fsdp')), may hold values from 0 to 1, as said below
- padding: int32 [38080], P(('dp', 'fsdp')), may hold values from 0 to 1, as said below
- qkv_weight: float32 [768, 2304], P(('dp', 'fsdp')), may hold values from -0.21875 to 0.21875
- qkv_moment: float32 [768, 2304], P(('dp', 'fsdp')), may hold values from -702.5075 to 702.5075
- qkv_average: float32 [768, 2304], P(('dp', 'fsdp')), may hold values from -0.21875 to 0.21875
- merge_weight: float32 [768, 768], P(('dp', 'fsdp')), may hold values from -2.5 to 2.5
- merge_moment: float32 [768, 768], P(('dp', 'fsdp')), may hold values from -81.959206 to 81.959206
- merge_average: float32 [768, 768], P(('dp', 'fsdp')), may hold values from -2.5 to 2.5
- expand_weight: float32 [768, 3072], P(('dp', 'fsdp')), may hold values from -0.21875 to 0.21875
- expand_moment: float32 [768, 3072], P(('dp', 'fsdp')), may hold values from -351.25375 to 351.25375
- expand_average: float32 [768, 3072], P(('dp', 'fsdp')), may hold values from -0.21875 to 0.21875
- shrink_weight: float32 [3072, 768], P(('dp', 'fsdp')), may hold values from -0.109375 to 0.109375
- shrink_moment: float32 [3072, 768], P(('dp', 'fsdp')), may hold values from -702.5075 to 702.5075
- shrink_average: float32 [3072, 768], P(('dp', 'fsdp')), may hold values from -0.109375 to 0.109375
- small_params: float32 [9216], P(('dp', 'fsdp')), may hold values from -0.4 to 1.4
- small_moment: float32 [9216], P(('dp', 'fsdp')), may hold values from -585.4229 to 585.4229
- small_average: float32 [9216], P(('dp', 'fsdp')), may hold values from -0.4 to 1.4
Outputs:
- activations: bfloat16 [38080, 768], P(('dp', 'fsdp'))
- input_grad: float32 [38080, 768], P(('dp', 'fsdp'))
- qkv_grad: float32 [768, 2304], P(('dp', 'fsdp'))
- qkv_newmoment: float32 [768, 2304], P(('dp', 'fsdp'))
- qkv_updated: float32 [768, 2304], P(('dp', 'fsdp'))
- qkv_newaverage: float32 [768, 2304], P(('dp', 'fsdp'))
- qkv_lowcopy: bfloat16 [768, 2304], P(('dp', 'fsdp'))
- merge_grad: float32 [768, 768], P(('dp', 'fsdp'))
- merge_newmoment: float32 [768, 768], P(('dp', 'fsdp'))
- merge_updated: float32 [768, 768], P(('dp', 'fsdp'))
- merge_newaverage: float32 [768, 768], P(('dp', 'fsdp'))
- merge_lowcopy: bfloat16 [768, 768], P(('dp', 'fsdp'))
- expand_grad: float32 [768, 3072], P(('dp', 'fsdp'))
- expand_newmoment: float32 [768, 3072], P(('dp', 'fsdp'))
- expand_updated: float32 [768, 3072], P(('dp', 'fsdp'))
- expand_newaverage: float32 [768, 3072], P(('dp', 'fsdp'))
- expand_lowcopy: bfloat16 [768, 3072], P(('dp', 'fsdp'))
- shrink_grad: float32 [3072, 768], P(('dp', 'fsdp'))
- shrink_newmoment: float32 [3072, 768], P(('dp', 'fsdp'))
- shrink_updated: float32 [3072, 768], P(('dp', 'fsdp'))
- shrink_newaverage: float32 [3072, 768], P(('dp', 'fsdp'))
- shrink_lowcopy: bfloat16 [3072, 768], P(('dp', 'fsdp'))
- small_grad: float32 [9216], P(('dp', 'fsdp'))
- small_newmoment: float32 [9216], P(('dp', 'fsdp'))
- small_updated: float32 [9216], P(('dp', 'fsdp'))
- small_newaverage: float32 [9216], P(('dp', 'fsdp'))
- small_lowcopy: bfloat16 [9216], P(('dp', 'fsdp'))
The draws below stay inside these ranges and needn't reach their ends.
Inputs may be any that keep to these rules, and one draw needn't show every extreme that they name: `segments`: on a quarter of the devices, drawn from the seed, all 1190 slots have segment 0 (one full clip). On every other device slots 0 to 471 have segment 0 and the slots from 472 on have segment 1. `padding`: on the full-clip devices of segments every slot is 1; on the others the first 944 slots are 1 and the rest 0.
All inputs are finite; a program needn't handle non-finite values.
Results may differ from the reference program's by a relative error of at most 0.012.
Values may be sent and summed in bfloat16 or wider, within the bound.
A program may use at most 192 MiB of HBM per device.

```python
import jax
import jax.numpy as jnp
from jax import lax

D = 768
HEADS = 12
HEAD_DIM = 64
FF = 3072
SLOTS = 1190
SHORT = 472
TOKENS = 38080
N_DP = 2
N_FSDP = 16


def clip_layout(key):
    devices = TOKENS // SLOTS
    order = jax.random.permutation(jax.random.fold_in(key, 5), devices)
    long_clip = order < devices // 4
    places = jnp.arange(SLOTS, dtype=jnp.int32)
    return (long_clip, places)


def draw_segments(key, part):
    long_clip, places = clip_layout(key)
    later = (places >= SHORT).astype(jnp.int32)
    return jnp.where(long_clip[:, None], 0, later[None, :]).reshape(-1).astype(jnp.int32)


def draw_padding(key, part):
    long_clip, places = clip_layout(key)
    inside = (places < 2 * SHORT).astype(jnp.int32)
    return jnp.where(long_clip[:, None], 1, inside[None, :]).reshape(-1).astype(jnp.int32)


def small_layout(key):
    noise = jnp.clip(jax.random.normal(key, (8 * D + FF,), jnp.float32), -4.0, 4.0)
    places = jnp.arange(8 * D + FF, dtype=jnp.int32)
    vector_number = places % (8 + FF // D)
    is_gain = (vector_number == 0) | (vector_number == 5)
    spread = jnp.where(vector_number == 3, 0.05, 0.1)
    return jnp.where(is_gain, 1.0, 0.0) + spread * noise


def draw_small_params(key, part):
    return small_layout(jax.random.fold_in(key, 11))


def draw_small_average(key, part):
    return small_layout(jax.random.fold_in(key, 13))


def strengthened(array, own_key, source, target, shards_of, factor):
    def block_of(position):
        return (jnp.arange(array.shape[position]) // (array.shape[position] // shards_of)).reshape((-1,) + (1,) * (array.ndim - 1 - position))

    one_side = jax.random.permutation(own_key, shards_of)[block_of(target)]
    other_side = (block_of(target) + shards_of // 2) % shards_of
    return jnp.where((block_of(source) == one_side) | (block_of(source) == other_side), factor * array, array)


def block_levels(rng, shape, cuts, least, top_value):
    level = 1.0
    for axis_at, blocks in cuts:
        heights = jax.random.uniform(jax.random.fold_in(jax.random.fold_in(rng, 6), axis_at), (blocks,), jnp.float32, least / len(cuts), top_value / len(cuts))
        level = level * jnp.repeat(jnp.exp(heights), shape[axis_at] // blocks).reshape((-1,) + (1,) * (len(shape) - 1 - axis_at))
    return level


def bell_draw(own_key, shape, deviation, limit, split=(), kind=jnp.bfloat16):
    loudness = block_levels(own_key, shape, split, -0.22, 0.18) if split else 1.0
    values = jax.random.normal(own_key, shape, jnp.float32) * deviation * loudness
    return jnp.minimum(jnp.maximum(values, -limit), limit).astype(kind)


def noise_with(rng, extent, deviation, reach, cuts, heavy, held_as=jnp.bfloat16):
    values = deviation * jax.random.normal(rng, extent, jnp.float32)
    if cuts:
        values = values * block_levels(rng, extent, cuts, -0.22, 0.18)
    return jnp.clip(strengthened(values, jax.random.fold_in(rng, 3), *heavy), -reach, reach).astype(held_as)


def setup_inputs(seed: int = 0) -> dict:
    key_of = jax.random.split(jax.random.key(seed), 20)
    return {
        "tokens": noise_with(key_of[0], (TOKENS, D), 1.0, 6.0, ((0, 32),), (0, 1, 32, 2.75)),
        "cotangent": bell_draw(key_of[1], (TOKENS, D), 1.0, 6.0, ((0, 32),)),
        "segments": draw_segments(jax.random.fold_in(key_of[19], 71), 0),
        "padding": draw_padding(jax.random.fold_in(key_of[19], 71), 0),
        "qkv_weight": bell_draw(key_of[4], (D, 3 * D), D ** -0.5, 0.21875, ((0, 32),), jnp.float32),
        "qkv_moment": bell_draw(key_of[5], (D, 3 * D), (0.6 * TOKENS ** 0.5), 702.5075, ((0, 32),), jnp.float32),
        "qkv_average": bell_draw(key_of[6], (D, 3 * D), D ** -0.5, 0.21875, ((0, 32),), jnp.float32),
        "merge_weight": bell_draw(key_of[7], (D, D), (D // 128) ** -0.5, 2.5, ((0, 32),), jnp.float32),
        "merge_moment": bell_draw(key_of[8], (D, D), (0.07 * TOKENS ** 0.5), 81.959206, ((0, 32),), jnp.float32),
        "merge_average": bell_draw(key_of[9], (D, D), (D // 128) ** -0.5, 2.5, ((0, 32),), jnp.float32),
        "expand_weight": bell_draw(key_of[10], (D, FF), D ** -0.5, 0.21875, ((0, 32),), jnp.float32),
        "expand_moment": bell_draw(key_of[11], (D, FF), (0.3 * TOKENS ** 0.5), 351.25375, ((0, 32),), jnp.float32),
        "expand_average": bell_draw(key_of[12], (D, FF), D ** -0.5, 0.21875, ((0, 32),), jnp.float32),
        "shrink_weight": bell_draw(key_of[13], (FF, D), FF ** -0.5, 0.109375, ((0, 32),), jnp.float32),
        "shrink_moment": bell_draw(key_of[14], (FF, D), (0.6 * TOKENS ** 0.5), 702.5075, ((0, 32),), jnp.float32),
        "shrink_average": bell_draw(key_of[15], (FF, D), FF ** -0.5, 0.109375, ((0, 32),), jnp.float32),
        "small_params": draw_small_params(jax.random.fold_in(key_of[19], 71), 0),
        "small_moment": bell_draw(key_of[17], (8 * D + FF,), (0.5 * TOKENS ** 0.5), 585.4229, ((0, 32),), jnp.float32),
        "small_average": draw_small_average(jax.random.fold_in(key_of[19], 71), 0),
    }


@jax.custom_vjp
def low(v):
    return lax.optimization_barrier(v.astype(jnp.bfloat16)).astype(jnp.float32)

@jax.custom_vjp
def low_back(v):
    return v

def low_keep(v):
    return (low(v), None)

def low_pass(kept, grad):
    return (grad,)

def back_keep(v):
    return (v, None)

def back_low(kept, grad):
    return (low(grad),)
low.defvjp(low_keep, low_pass)
low_back.defvjp(back_keep, back_low)
epsilon = 1e-06
highest = lax.Precision.HIGHEST

def normalize(values, gain_vector, shift_vector):
    centred = values - lax.optimization_barrier(jnp.mean(values, axis=-1, keepdims=True))
    spread = lax.optimization_barrier(jnp.mean(centred * centred, axis=-1, keepdims=True))
    return centred * lax.rsqrt(spread + epsilon) * gain_vector + shift_vector

def attend(queries, keyset, valueset, allowed):
    slots = queries.shape[0]

    def split_heads(values):
        return values.reshape(slots, HEADS // 2, 2, HEAD_DIM).transpose(1, 0, 2, 3)

    def one_pair(pieces):
        query_pair, key_pair, value_pair = pieces
        scores = jnp.einsum('qhd,khd->hqk', query_pair, key_pair, precision=highest) * HEAD_DIM ** (-0.5)
        scores = low_back(scores)
        masked = jnp.where(allowed[None], scores, -1e+30)
        weights = low(jax.nn.softmax(masked, axis=-1))
        return jnp.einsum('hqk,khd->qhd', weights, value_pair, precision=highest)
    results = lax.map(jax.checkpoint(one_pair), (split_heads(queries), split_heads(keyset), split_heads(valueset)))
    return results.transpose(1, 0, 2, 3).reshape(slots, HEADS * HEAD_DIM)

def forward(inputs, allowed, qkv_master, merge_master, expand_master, shrink_master, small_master):
    vectors = low(small_master).reshape(D, 8 + FF // D)
    pieces = [vectors[:, number] for number in range(8)]
    gain_one, shift_one, bias_query, bias_value, bias_merge, gain_two, shift_two, bias_shrink = pieces
    bias_expand = vectors[:, 8:].T.reshape(FF)
    norm_one = low(normalize(inputs, gain_one, shift_one))
    joined = jnp.dot(norm_one, low(qkv_master), precision=highest)
    joined = joined + jnp.concatenate([bias_query, jnp.zeros((D,), jnp.float32), bias_value])
    joined = low(low_back(joined))
    attended = attend(joined[:, :D], joined[:, D:2 * D], joined[:, 2 * D:], allowed)
    attended = low(low_back(attended))
    middle = inputs + low_back(jnp.dot(attended, low(merge_master), precision=highest) + bias_merge)
    norm_two = low(normalize(middle, gain_two, shift_two))
    before = low_back(jnp.dot(norm_two, low(expand_master), precision=highest) + bias_expand)
    after_low = low(jax.nn.gelu(before, approximate=False))
    return middle + low_back(jnp.dot(after_low, low(shrink_master), precision=highest) + bias_shrink)

def reference(tokens, cotangent, segments, padding, qkv_weight, qkv_moment, qkv_average, merge_weight, merge_moment, merge_average, expand_weight, expand_moment, expand_average, shrink_weight, shrink_moment, shrink_average, small_params, small_moment, small_average):
    devices = N_DP * N_FSDP
    masters = (qkv_weight, merge_weight, expand_weight, shrink_weight, small_params)
    blocks = (tokens.reshape(devices, SLOTS, D), cotangent.reshape(devices, SLOTS, D), segments.reshape(devices, SLOTS), padding.reshape(devices, SLOTS))

    def one_device(running, device_block):
        inputs, incoming, labels, valid_rows = device_block
        allowed = (labels[:, None] == labels[None, :]) & (valid_rows[:, None] == valid_rows[None, :])

        def on_device(values, *weights):
            return forward(values, allowed, *weights)
        result, backward = jax.vjp(on_device, inputs.astype(jnp.float32), *masters)
        weighted = incoming.astype(jnp.float32) * valid_rows[:, None].astype(jnp.float32)
        gradients = backward(weighted)
        running = tuple((summed + gradient for summed, gradient in zip(running, gradients[1:])))
        return (running, (result.astype(jnp.bfloat16), gradients[0]))
    starting = tuple((jnp.zeros_like(master) for master in masters))
    totals, (outputs, input_grads) = lax.scan(one_device, starting, blocks)
    rate_scale = TOKENS ** (-0.5)
    rates = (0.04 * rate_scale, 4.0 * rate_scale, 0.08 * rate_scale, 0.02 * rate_scale, 0.07 * rate_scale)
    moments = (qkv_moment, merge_moment, expand_moment, shrink_moment, small_moment)
    averages = (qkv_average, merge_average, expand_average, shrink_average, small_average)
    updates = []
    for master, gradient, moment, average, step_rate in zip(masters, totals, moments, averages, rates):
        fresh_moment = 0.5 * moment + gradient
        updated = master - step_rate * (gradient + 0.5 * fresh_moment)
        updates.append((gradient, fresh_moment, updated, 0.5 * average + 0.5 * updated, updated.astype(jnp.bfloat16)))
    return (outputs.reshape(TOKENS, D), input_grads.reshape(TOKENS, D), updates[0][0], updates[0][1], updates[0][2], updates[0][3], updates[0][4], updates[1][0], updates[1][1], updates[1][2], updates[1][3], updates[1][4], updates[2][0], updates[2][1], updates[2][2], updates[2][3], updates[2][4], updates[3][0], updates[3][1], updates[3][2], updates[3][3], updates[3][4], updates[4][0], updates[4][1], updates[4][2], updates[4][3], updates[4][4])
```

```python
from functools import partial
import jax, jax.numpy as jnp
from jax import lax
from jax.sharding import PartitionSpec as P
from jax.experimental import pallas as pl
from jax.experimental.pallas import tpu as pltpu

HEAD_DIM = 64
BIG = 2.0 ** 100
F32 = jnp.float32
BF16 = jnp.bfloat16


def round_up(n, m):
    return (n + m - 1) // m * m


def mask_features(segments, padding, slots):
    wide = round_up(slots, 256)
    group = segments * 2 + padding
    group = jnp.concatenate([group, jnp.full((wide - slots,), 4, jnp.int32)])[:, None]
    lane = lax.broadcasted_iota(jnp.int32, (wide, 128), 1) % HEAD_DIM
    same = group == lane
    query_side = jnp.where((lane < 5) & ~same, -BIG, 0.0).astype(BF16)
    key_side = jnp.where(same | ((lane >= 5) & (lane < 8)), 1.0, 0.0).astype(BF16)
    return query_side, key_side


def dot_nt(a, b):
    return lax.dot_general(a, b, (((1,), (1,)), ((), ())), preferred_element_type=F32)


def dot_nn(a, b):
    return lax.dot_general(a, b, (((1,), (0,)), ((), ())), preferred_element_type=F32)


def dot_tn(a, b):
    return lax.dot_general(a, b, (((0,), (0,)), ((), ())), preferred_element_type=F32)


def fill(target, value, features, keep_low, slots):
    wide = target.shape[0]
    start = slots // 16 * 16
    low_half = lax.broadcasted_iota(jnp.int32, (wide - start, 128), 1) < HEAD_DIM
    tail = features[start:wide, :] if features is not None else jnp.ones((wide - start, 128), BF16)
    target[start:wide, :] = jnp.where(low_half == keep_low, jnp.zeros_like(tail), tail)
    target[0:slots, :] = value


def forward_kernel(slots, block, q_ref, k_ref, v_ref, fq_ref, fk_ref,
                   low_ref, wide_ref, lse_ref, qa, qb, ka, kb, va, vb, out, lse):
    low_half = lax.broadcasted_iota(jnp.int32, (slots, 128), 1) < HEAD_DIM
    q = q_ref[...] * 0.125
    fq = fq_ref[0:slots, :]
    fk = fk_ref[0:slots, :]
    fill(qa, jnp.where(low_half, q, fq), fq_ref, True, slots)
    fill(qb, jnp.where(low_half, fq, q), fq_ref, False, slots)
    k = k_ref[...]
    fill(ka, jnp.where(low_half, k, fk), fk_ref, True, slots)
    fill(kb, jnp.where(low_half, fk, k), fk_ref, False, slots)
    v = v_ref[...]
    one = jnp.ones_like(v)
    fill(va, jnp.where(low_half, v, one), None, True, slots)
    fill(vb, jnp.where(low_half, one, v), None, False, slots)
    half = lax.broadcasted_iota(jnp.int32, (block, 128), 1) < HEAD_DIM

    def head(qx, kx, vx, rows):
        scores = dot_nt(qx[rows, :], kx[...])
        top = jnp.max(scores, axis=1, keepdims=True)
        weights = jnp.exp(scores - top).astype(BF16)
        return dot_nn(weights, vx[...]), top

    def step(number, carry):
        rows = pl.ds(pl.multiple_of(number * block, 16), block)
        raw_a, top_a = head(qa, ka, va, rows)
        raw_b, top_b = head(qb, kb, vb, rows)
        sums = jnp.where(half, raw_b, raw_a)
        lse[rows, :] = jnp.where(half, top_b, top_a) + jnp.log(sums)
        out[rows, :] = jnp.where(half, raw_a, raw_b) / pltpu.roll(sums, HEAD_DIM, 1)
        return carry

    lax.fori_loop(0, out.shape[0] // block, step, 0)
    attended = out[0:slots, :]
    low_ref[...] = attended.astype(BF16)
    wide_ref[...] = attended
    lse_ref[...] = lse[0:slots, :]


def column(shift, slots):
    return pl.BlockSpec((slots, 128), lambda p, s=shift: (0, s + p))


def attention_forward(qkv, fq, fk, block=240):
    slots = qkv.shape[0]
    pairs = qkv.shape[1] // 384
    wide = fq.shape[0]
    rows = round_up(slots, block)
    whole = pl.BlockSpec((wide, 128), lambda p: (0, 0))
    width = pairs * 128
    return pl.pallas_call(
        partial(forward_kernel, slots, block),
        grid=(pairs,),
        in_specs=[column(0, slots), column(pairs, slots), column(2 * pairs, slots), whole, whole],
        out_specs=[column(0, slots)] * 3,
        out_shape=[
            jax.ShapeDtypeStruct((slots, width), BF16),
            jax.ShapeDtypeStruct((slots, width), F32),
            jax.ShapeDtypeStruct((slots, width), F32),
        ],
        scratch_shapes=[pltpu.VMEM((wide, 128), BF16)] * 6 + [pltpu.VMEM((rows, 128), F32)] * 2,
        compiler_params=pltpu.CompilerParams(vmem_limit_bytes=50 * 2 ** 20),
        name="attention_forward",
    )(qkv, qkv, qkv, fq, fk)


def thirds(value):
    high = value.astype(BF16)
    rest = value - high.astype(F32)
    mid = rest.astype(BF16)
    return high, mid, (rest - mid.astype(F32)).astype(BF16)


def backward_kernel(slots, block, q_ref, k_ref, v_ref, g_ref, wide_ref, lse_ref, fq_ref, fk_ref,
                    dq_ref, dk_ref, dv_ref, qa, qb, ka, kb, va, vb, ga, gb, dqa, dqb, dk, dv):
    lane = lax.broadcasted_iota(jnp.int32, (slots, 128), 1)
    low_half = lane < HEAD_DIM
    spot = lane % HEAD_DIM
    q = q_ref[...] * 0.125
    fk = fk_ref[0:slots, :]
    high, mid, low = thirds(-lse_ref[...])
    fq = jnp.where(spot == 5, high, jnp.where(spot == 6, mid, jnp.where(spot == 7, low, fq_ref[0:slots, :])))
    fill(qa, jnp.where(low_half, q, fq), fq_ref, True, slots)
    fill(qb, jnp.where(low_half, fq, q), fq_ref, False, slots)
    k = k_ref[...]
    fill(ka, jnp.where(low_half, k, fk), fk_ref, True, slots)
    fill(kb, jnp.where(low_half, fk, k), fk_ref, False, slots)
    v = v_ref[...]
    one = jnp.ones_like(v)
    fill(va, jnp.where(low_half, v, one), None, True, slots)
    fill(vb, jnp.where(low_half, one, v), None, False, slots)
    g = g_ref[...]
    product = g.astype(F32) * wide_ref[...]
    delta_a = jnp.sum(jnp.where(low_half, product, 0.0), axis=1, keepdims=True)
    delta_b = jnp.sum(jnp.where(low_half, 0.0, product), axis=1, keepdims=True)
    high, mid, low = thirds(-jnp.where(low_half, delta_b, delta_a))
    zero = jnp.zeros_like(g)
    fg = jnp.where(spot == 0, high, jnp.where(spot == 1, mid, jnp.where(spot == 2, low, zero)))
    ga[...] = jnp.zeros_like(ga)
    gb[...] = jnp.zeros_like(gb)
    ga[0:slots, :] = jnp.where(low_half, g, fg)
    gb[0:slots, :] = jnp.where(low_half, fg, g)
    dqa[...] = jnp.zeros_like(dqa)
    dqb[...] = jnp.zeros_like(dqb)
    half = lax.broadcasted_iota(jnp.int32, (block, 128), 1) < HEAD_DIM

    def head(qx, kx, vx, gx, dqx, rows):
        keys = kx[rows, :]
        probs = jnp.exp(dot_nt(keys, qx[...]))
        value_grad = dot_nn(probs.astype(BF16), gx[...])
        score_grad = (probs * dot_nt(vx[rows, :], gx[...])).astype(BF16)
        key_grad = dot_nn(score_grad, qx[...])
        dqx[...] += dot_tn(score_grad, keys)
        return key_grad, value_grad

    def step(number, carry):
        rows = pl.ds(pl.multiple_of(number * block, 16), block)
        key_a, value_a = head(qa, ka, va, ga, dqa, rows)
        key_b, value_b = head(qb, kb, vb, gb, dqb, rows)
        dk[rows, :] = jnp.where(half, key_a, key_b)
        dv[rows, :] = jnp.where(half, value_a, value_b)
        return carry

    lax.fori_loop(0, dk.shape[0] // block, step, 0)
    dq_ref[...] = (jnp.where(low_half, dqa[0:slots, :], dqb[0:slots, :]) * 0.125).astype(BF16)
    dk_ref[...] = dk[0:slots, :].astype(BF16)
    dv_ref[...] = dv[0:slots, :].astype(BF16)


def attention_backward(qkv, upstream, wide_out, lse, fq, fk, block=240):
    slots = qkv.shape[0]
    pairs = qkv.shape[1] // 384
    wide = fq.shape[0]
    rows = round_up(slots, block)
    whole = pl.BlockSpec((wide, 128), lambda p: (0, 0))
    width = pairs * 128
    return pl.pallas_call(
        partial(backward_kernel, slots, block),
        grid=(pairs,),
        in_specs=[column(0, slots), column(pairs, slots), column(2 * pairs, slots),
                  column(0, slots), column(0, slots), column(0, slots), whole, whole],
        out_specs=[column(0, slots)] * 3,
        out_shape=[jax.ShapeDtypeStruct((slots, width), BF16)] * 3,
        scratch_shapes=[pltpu.VMEM((wide, 128), BF16)] * 8
        + [pltpu.VMEM((wide, 128), F32)] * 2 + [pltpu.VMEM((rows, 128), F32)] * 2,
        compiler_params=pltpu.CompilerParams(vmem_limit_bytes=60 * 2 ** 20),
        name="attention_backward",
    )(qkv, qkv, qkv, upstream, wide_out, lse, fq, fk)


D = 768
FF = 3072


epsilon = 1e-06
root_half = 0.7071067811865476
inverse_root_tau = 0.3989422804014327


def normalize_keep(values, gain_vector, shift_vector):
    centred = values - jnp.mean(values, axis=-1, keepdims=True)
    inverse = lax.rsqrt(jnp.mean(centred * centred, axis=-1, keepdims=True) + epsilon)
    scaled = centred * inverse
    return (scaled * gain_vector + shift_vector, scaled, inverse)


def normalize_back(upstream, scaled, inverse, gain_vector):
    weighted = upstream * gain_vector
    centred = weighted - jnp.mean(weighted, axis=-1, keepdims=True)
    result = inverse * (centred - scaled * jnp.mean(weighted * scaled, axis=-1, keepdims=True))
    return (result, jnp.sum(upstream * scaled, axis=0), jnp.sum(upstream, axis=0))


def split_vectors(small_full):
    columns = small_full.astype(jnp.float32)
    pieces = [columns[:, number] for number in range(8)]
    return (pieces, columns[:, 8:].T.reshape(FF))


def per_device(
    tokens,
    cotangent,
    segments,
    padding,
    qkv_weight,
    qkv_moment,
    qkv_average,
    merge_weight,
    merge_moment,
    merge_average,
    expand_weight,
    expand_moment,
    expand_average,
    shrink_weight,
    shrink_moment,
    shrink_average,
    small_params,
    small_moment,
    small_average,
):
    masters = (qkv_weight, merge_weight, expand_weight, shrink_weight, small_params)
    lowered = tuple((master.astype(jnp.bfloat16) for master in masters))
    low_qkv, low_merge, low_expand, low_shrink, low_small = lowered
    axes = ("dp", "fsdp")
    own_rows = qkv_weight.shape[0]
    first = jnp.concatenate([low_qkv, low_small.reshape(own_rows, -1)], axis=1)
    first = lax.all_gather(first, axes, axis=0, tiled=True)
    second = jnp.concatenate([low_merge, low_expand], axis=1)
    second = lax.all_gather(second, axes, axis=0, tiled=True)
    shrink_full = lax.all_gather(low_shrink, axes, axis=0, tiled=True)
    qkv_full, small_full = first[:, : 3 * D], first[:, 3 * D :]
    merge_full, expand_full = second[:, :D], second[:, D:]
    pieces, bias_expand = split_vectors(small_full)
    gain_one, shift_one, bias_query, bias_value, bias_merge, gain_two, shift_two, bias_shrink = (
        pieces
    )
    inputs = tokens.astype(jnp.float32)
    query_mask, key_mask = mask_features(segments, padding, tokens.shape[0])
    norm_one, scaled_one, inverse_one = normalize_keep(inputs, gain_one, shift_one)
    norm_one_low = norm_one.astype(jnp.bfloat16)
    joined = jnp.dot(norm_one_low, qkv_full, preferred_element_type=jnp.float32)
    joined = joined + jnp.concatenate([bias_query, jnp.zeros((D,), jnp.float32), bias_value])
    joined_low = joined.astype(jnp.bfloat16)
    attended_low, attended_wide, logsums = attention_forward(joined_low, query_mask, key_mask)
    middle = (
        inputs + jnp.dot(attended_low, merge_full, preferred_element_type=jnp.float32) + bias_merge
    )
    norm_two, scaled_two, inverse_two = normalize_keep(middle, gain_two, shift_two)
    norm_two_low = norm_two.astype(jnp.bfloat16)
    before = jnp.dot(norm_two_low, expand_full, preferred_element_type=jnp.float32) + bias_expand
    after_low = jax.nn.gelu(before, approximate=False).astype(jnp.bfloat16)
    output = (
        middle + jnp.dot(after_low, shrink_full, preferred_element_type=jnp.float32) + bias_shrink
    )
    activations = output.astype(jnp.bfloat16)
    back_gain_one, back_gain_two = gain_one, gain_two
    outgoing = cotangent.astype(jnp.float32) * padding[:, None].astype(jnp.float32)
    outgoing_low = outgoing.astype(jnp.bfloat16)
    shrink_part = jnp.einsum(
        "sf,sd->fd", after_low, outgoing_low, preferred_element_type=jnp.float32
    )
    shrink_bias_part = jnp.sum(outgoing, axis=0)
    act_grad = jnp.einsum(
        "sd,fd->sf", outgoing_low, shrink_full, preferred_element_type=jnp.float32
    )
    cumulative = 0.5 * (1.0 + lax.erf(before * root_half))
    density = jnp.exp(-0.5 * before * before) * inverse_root_tau
    before_grad = (act_grad * (cumulative + before * density)).astype(jnp.bfloat16)
    expand_part = jnp.einsum(
        "sd,sf->df", norm_two_low, before_grad, preferred_element_type=jnp.float32
    )
    expand_bias_part = jnp.sum(before_grad.astype(jnp.float32), axis=0)
    up_two = jnp.einsum("sf,df->sd", before_grad, expand_full, preferred_element_type=jnp.float32)
    second_back, gain_two_part, shift_two_part = normalize_back(
        up_two, scaled_two, inverse_two, back_gain_two
    )
    middle_grad = outgoing + second_back
    middle_low = middle_grad.astype(jnp.bfloat16)
    merge_part = jnp.einsum(
        "sd,se->de", attended_low, middle_low, preferred_element_type=jnp.float32
    )
    merge_bias_part = jnp.sum(middle_low.astype(jnp.float32), axis=0)
    attended_grad = jnp.einsum(
        "se,de->sd", middle_low, merge_full, preferred_element_type=jnp.float32
    ).astype(jnp.bfloat16)
    query_grads, key_grads, value_grads = attention_backward(
        joined_low, attended_grad, attended_wide, logsums, query_mask, key_mask
    )
    qkv_grad_low = jnp.concatenate([query_grads, key_grads, value_grads], axis=1)
    qkv_part = jnp.einsum(
        "sd,sc->dc", norm_one_low, qkv_grad_low, preferred_element_type=jnp.float32
    )
    column_sums = jnp.sum(qkv_grad_low.astype(jnp.float32), axis=0)
    up_one = jnp.einsum("sc,dc->sd", qkv_grad_low, qkv_full, preferred_element_type=jnp.float32)
    first_back, gain_one_part, shift_one_part = normalize_back(
        up_one, scaled_one, inverse_one, back_gain_one
    )
    input_grad = middle_grad + first_back
    vector_rows = jnp.stack(
        [
            gain_one_part,
            shift_one_part,
            column_sums[:D],
            column_sums[2 * D :],
            merge_bias_part,
            gain_two_part,
            shift_two_part,
            shrink_bias_part,
        ]
    )
    all_rows = jnp.concatenate([vector_rows, expand_bias_part.reshape(FF // D, D)], axis=0)
    small_part = all_rows.T
    wide_part = jnp.concatenate([merge_part, expand_part], axis=1).astype(BF16)
    last_part = jnp.concatenate([qkv_part, small_part], axis=1).astype(BF16)
    shrink_sum = lax.psum_scatter(shrink_part.astype(BF16), axes, scatter_dimension=0, tiled=True)
    wide_sum = lax.psum_scatter(wide_part, axes, scatter_dimension=0, tiled=True).astype(F32)
    last_sum = lax.psum_scatter(last_part, axes, scatter_dimension=0, tiled=True).astype(F32)
    summed = (
        last_sum[:, : 3 * D],
        wide_sum[:, :D],
        wide_sum[:, D:],
        shrink_sum.astype(F32),
        last_sum[:, 3 * D :].reshape(-1),
    )
    rate_scale = (tokens.shape[0] * lax.axis_size("dp") * lax.axis_size("fsdp")) ** (-0.5)
    rates = (
        0.04 * rate_scale,
        4.0 * rate_scale,
        0.08 * rate_scale,
        0.02 * rate_scale,
        0.07 * rate_scale,
    )
    moments = (qkv_moment, merge_moment, expand_moment, shrink_moment, small_moment)
    averages = (qkv_average, merge_average, expand_average, shrink_average, small_average)
    results = [activations, input_grad]
    for master, gradient, moment, average, step_rate in zip(
        masters, summed, moments, averages, rates
    ):
        fresh_moment = 0.5 * moment + gradient
        updated = master - step_rate * (gradient + 0.5 * fresh_moment)
        results.extend(
            [
                gradient,
                fresh_moment,
                updated,
                0.5 * average + 0.5 * updated,
                updated.astype(jnp.bfloat16),
            ]
        )
    return tuple(results)


def solution(mesh):
    placed = (
        P(("dp", "fsdp"), None),
        P(("dp", "fsdp"), None),
        P(("dp", "fsdp")),
        P(("dp", "fsdp")),
        P(("dp", "fsdp"), None),
        P(("dp", "fsdp"), None),
        P(("dp", "fsdp"), None),
        P(("dp", "fsdp"), None),
        P(("dp", "fsdp"), None),
        P(("dp", "fsdp"), None),
        P(("dp", "fsdp"), None),
        P(("dp", "fsdp"), None),
        P(("dp", "fsdp"), None),
        P(("dp", "fsdp"), None),
        P(("dp", "fsdp"), None),
        P(("dp", "fsdp"), None),
        P(("dp", "fsdp")),
        P(("dp", "fsdp")),
        P(("dp", "fsdp")),
    )
    return jax.shard_map(
        per_device,
        mesh=mesh,
        in_specs=placed,
        out_specs=(
            P(("dp", "fsdp"), None),
            P(("dp", "fsdp"), None),
            P(("dp", "fsdp"), None),
            P(("dp", "fsdp"), None),
            P(("dp", "fsdp"), None),
            P(("dp", "fsdp"), None),
            P(("dp", "fsdp"), None),
            P(("dp", "fsdp"), None),
            P(("dp", "fsdp"), None),
            P(("dp", "fsdp"), None),
            P(("dp", "fsdp"), None),
            P(("dp", "fsdp"), None),
            P(("dp", "fsdp"), None),
            P(("dp", "fsdp"), None),
            P(("dp", "fsdp"), None),
            P(("dp", "fsdp"), None),
            P(("dp", "fsdp"), None),
            P(("dp", "fsdp"), None),
            P(("dp", "fsdp"), None),
            P(("dp", "fsdp"), None),
            P(("dp", "fsdp"), None),
            P(("dp", "fsdp"), None),
            P(("dp", "fsdp")),
            P(("dp", "fsdp")),
            P(("dp", "fsdp")),
            P(("dp", "fsdp")),
            P(("dp", "fsdp")),
        ),
        check_vma=False,
    )
```

```python
from functools import partial
import jax, jax.numpy as jnp
from jax import lax
from jax.sharding import PartitionSpec as P
from jax.experimental import pallas as pl
from jax.experimental.pallas import tpu as pltpu

HEAD_DIM = 64
BIG = 2.0 ** 100
F32 = jnp.float32
BF16 = jnp.bfloat16


def round_up(n, m):
    return (n + m - 1) // m * m


def mask_features(segments, padding, slots):
    wide = round_up(slots, 256)
    group = segments * 2 + padding
    group = jnp.concatenate([group, jnp.full((wide - slots,), 4, jnp.int32)])[:, None]
    lane = lax.broadcasted_iota(jnp.int32, (wide, 128), 1) % HEAD_DIM
    same = group == lane
    query_side = jnp.where((lane < 5) & ~same, -BIG, 0.0).astype(BF16)
    key_side = jnp.where(same | ((lane >= 5) & (lane < 8)), 1.0, 0.0).astype(BF16)
    return query_side, key_side


def dot_nt(a, b):
    return lax.dot_general(a, b, (((1,), (1,)), ((), ())), preferred_element_type=F32)


def dot_nn(a, b):
    return lax.dot_general(a, b, (((1,), (0,)), ((), ())), preferred_element_type=F32)


def dot_tn(a, b):
    return lax.dot_general(a, b, (((0,), (0,)), ((), ())), preferred_element_type=F32)


def fill(target, value, features, keep_low, slots):
    wide = target.shape[0]
    start = slots // 16 * 16
    low_half = lax.broadcasted_iota(jnp.int32, (wide - start, 128), 1) < HEAD_DIM
    tail = features[start:wide, :] if features is not None else jnp.ones((wide - start, 128), BF16)
    target[start:wide, :] = jnp.where(low_half == keep_low, jnp.zeros_like(tail), tail)
    target[0:slots, :] = value


def forward_kernel(slots, block, q_ref, k_ref, v_ref, fq_ref, fk_ref,
                   low_ref, wide_ref, lse_ref, qa, qb, ka, kb, va, vb, out, lse):
    low_half = lax.broadcasted_iota(jnp.int32, (slots, 128), 1) < HEAD_DIM
    q = q_ref[...] * 0.125
    fq = fq_ref[0:slots, :]
    fk = fk_ref[0:slots, :]
    fill(qa, jnp.where(low_half, q, fq), fq_ref, True, slots)
    fill(qb, jnp.where(low_half, fq, q), fq_ref, False, slots)
    k = k_ref[...]
    fill(ka, jnp.where(low_half, k, fk), fk_ref, True, slots)
    fill(kb, jnp.where(low_half, fk, k), fk_ref, False, slots)
    v = v_ref[...]
    one = jnp.ones_like(v)
    fill(va, jnp.where(low_half, v, one), None, True, slots)
    fill(vb, jnp.where(low_half, one, v), None, False, slots)
    half = lax.broadcasted_iota(jnp.int32, (block, 128), 1) < HEAD_DIM

    def head(qx, kx, vx, rows):
        scores = dot_nt(qx[rows, :], kx[...])
        top = jnp.max(scores, axis=1, keepdims=True)
        weights = jnp.exp(scores - top).astype(BF16)
        return dot_nn(weights, vx[...]), top

    def step(number, carry):
        rows = pl.ds(pl.multiple_of(number * block, 16), block)
        raw_a, top_a = head(qa, ka, va, rows)
        raw_b, top_b = head(qb, kb, vb, rows)
        sums = jnp.where(half, raw_b, raw_a)
        lse[rows, :] = jnp.where(half, top_b, top_a) + jnp.log(sums)
        out[rows, :] = jnp.where(half, raw_a, raw_b) / pltpu.roll(sums, HEAD_DIM, 1)
        return carry

    lax.fori_loop(0, out.shape[0] // block, step, 0)
    attended = out[0:slots, :]
    low_ref[...] = attended.astype(BF16)
    wide_ref[...] = attended
    lse_ref[...] = lse[0:slots, :]


def column(shift, slots):
    return pl.BlockSpec((slots, 128), lambda p, s=shift: (0, s + p))


def attention_forward(qkv, fq, fk, block=240):
    slots = qkv.shape[0]
    pairs = qkv.shape[1] // 384
    wide = fq.shape[0]
    rows = round_up(slots, block)
    whole = pl.BlockSpec((wide, 128), lambda p: (0, 0))
    width = pairs * 128
    return pl.pallas_call(
        partial(forward_kernel, slots, block),
        grid=(pairs,),
        in_specs=[column(0, slots), column(pairs, slots), column(2 * pairs, slots), whole, whole],
        out_specs=[column(0, slots)] * 3,
        out_shape=[
            jax.ShapeDtypeStruct((slots, width), BF16),
            jax.ShapeDtypeStruct((slots, width), F32),
            jax.ShapeDtypeStruct((slots, width), F32),
        ],
        scratch_shapes=[pltpu.VMEM((wide, 128), BF16)] * 6 + [pltpu.VMEM((rows, 128), F32)] * 2,
        compiler_params=pltpu.CompilerParams(vmem_limit_bytes=50 * 2 ** 20),
        name="attention_forward",
    )(qkv, qkv, qkv, fq, fk)


def thirds(value):
    high = value.astype(BF16)
    rest = value - high.astype(F32)
    mid = rest.astype(BF16)
    return high, mid, (rest - mid.astype(F32)).astype(BF16)


def backward_kernel(slots, block, q_ref, k_ref, v_ref, g_ref, wide_ref, lse_ref, fq_ref, fk_ref,
                    dq_ref, dk_ref, dv_ref, qa, qb, ka, kb, va, vb, ga, gb, dqa, dqb, dk, dv):
    lane = lax.broadcasted_iota(jnp.int32, (slots, 128), 1)
    low_half = lane < HEAD_DIM
    spot = lane % HEAD_DIM
    q = q_ref[...] * 0.125
    fk = fk_ref[0:slots, :]
    high, mid, low = thirds(-lse_ref[...])
    fq = jnp.where(spot == 5, high, jnp.where(spot == 6, mid, jnp.where(spot == 7, low, fq_ref[0:slots, :])))
    fill(qa, jnp.where(low_half, q, fq), fq_ref, True, slots)
    fill(qb, jnp.where(low_half, fq, q), fq_ref, False, slots)
    k = k_ref[...]
    fill(ka, jnp.where(low_half, k, fk), fk_ref, True, slots)
    fill(kb, jnp.where(low_half, fk, k), fk_ref, False, slots)
    v = v_ref[...]
    one = jnp.ones_like(v)
    fill(va, jnp.where(low_half, v, one), None, True, slots)
    fill(vb, jnp.where(low_half, one, v), None, False, slots)
    g = g_ref[...]
    product = g.astype(F32) * wide_ref[...]
    delta_a = jnp.sum(jnp.where(low_half, product, 0.0), axis=1, keepdims=True)
    delta_b = jnp.sum(jnp.where(low_half, 0.0, product), axis=1, keepdims=True)
    high, mid, low = thirds(-jnp.where(low_half, delta_b, delta_a))
    zero = jnp.zeros_like(g)
    fg = jnp.where(spot == 0, high, jnp.where(spot == 1, mid, jnp.where(spot == 2, low, zero)))
    ga[...] = jnp.zeros_like(ga)
    gb[...] = jnp.zeros_like(gb)
    ga[0:slots, :] = jnp.where(low_half, g, fg)
    gb[0:slots, :] = jnp.where(low_half, fg, g)
    dqa[...] = jnp.zeros_like(dqa)
    dqb[...] = jnp.zeros_like(dqb)
    half = lax.broadcasted_iota(jnp.int32, (block, 128), 1) < HEAD_DIM

    def head(qx, kx, vx, gx, dqx, rows):
        keys = kx[rows, :]
        probs = jnp.exp(dot_nt(keys, qx[...]))
        value_grad = dot_nn(probs.astype(BF16), gx[...])
        score_grad = (probs * dot_nt(vx[rows, :], gx[...])).astype(BF16)
        key_grad = dot_nn(score_grad, qx[...])
        dqx[...] += dot_tn(score_grad, keys)
        return key_grad, value_grad

    def step(number, carry):
        rows = pl.ds(pl.multiple_of(number * block, 16), block)
        key_a, value_a = head(qa, ka, va, ga, dqa, rows)
        key_b, value_b = head(qb, kb, vb, gb, dqb, rows)
        dk[rows, :] = jnp.where(half, key_a, key_b)
        dv[rows, :] = jnp.where(half, value_a, value_b)
        return carry

    lax.fori_loop(0, dk.shape[0] // block, step, 0)
    dq_ref[...] = (jnp.where(low_half, dqa[0:slots, :], dqb[0:slots, :]) * 0.125).astype(BF16)
    dk_ref[...] = dk[0:slots, :].astype(BF16)
    dv_ref[...] = dv[0:slots, :].astype(BF16)


def attention_backward(qkv, upstream, wide_out, lse, fq, fk, block=240):
    slots = qkv.shape[0]
    pairs = qkv.shape[1] // 384
    wide = fq.shape[0]
    rows = round_up(slots, block)
    whole = pl.BlockSpec((wide, 128), lambda p: (0, 0))
    width = pairs * 128
    return pl.pallas_call(
        partial(backward_kernel, slots, block),
        grid=(pairs,),
        in_specs=[column(0, slots), column(pairs, slots), column(2 * pairs, slots),
                  column(0, slots), column(0, slots), column(0, slots), whole, whole],
        out_specs=[column(0, slots)] * 3,
        out_shape=[jax.ShapeDtypeStruct((slots, width), BF16)] * 3,
        scratch_shapes=[pltpu.VMEM((wide, 128), BF16)] * 8
        + [pltpu.VMEM((wide, 128), F32)] * 2 + [pltpu.VMEM((rows, 128), F32)] * 2,
        compiler_params=pltpu.CompilerParams(vmem_limit_bytes=60 * 2 ** 20),
        name="attention_backward",
    )(qkv, qkv, qkv, upstream, wide_out, lse, fq, fk)


MESH = pl.DeviceIdType.MESH


class Place:
    def __init__(self, n_dp, n_fsdp):
        self.n_dp, self.n_fsdp, self.lines = n_dp, n_fsdp, n_fsdp // 4
        self.dp, at = lax.axis_index("dp"), lax.axis_index("fsdp")
        core = self.dp % 2
        self.stride_u, self.stride_w = 2 - core, 1 + core
        high, low = (at // 2) % 2, at % 2
        self.a = at // 4
        self.u = high * (1 - core) + low * core
        self.w = low * (1 - core) + high * core

    def fsdp_of(self, da, du, dw):
        a, u, w = (self.a + da) % self.lines, (self.u + du) % 2, (self.w + dw) % 2
        return a * 4 + u * self.stride_u + w * self.stride_w

    def dp_of(self, dd):
        return (self.dp + dd) % self.n_dp

    def piece(self, dd, da, du, dw):
        return self.dp_of(dd) * self.n_fsdp + self.fsdp_of(da, du, dw)

    def device(self, dd, da, du, dw):
        return (self.dp_of(dd), self.fsdp_of(da, du, dw))

    def slot(self, dd, da, du, dw):
        return ((dd * self.lines + da) * 2 + du) * 2 + dw

    def greet(self):
        barrier = pltpu.get_barrier_semaphore()
        friends = [(0, 0, 1, 0), (0, 0, 0, 1)]
        friends += [(0, da, 0, 0) for da in range(1, self.lines)]
        friends += [(dd, 0, 0, 0) for dd in range(1, self.n_dp)]
        for friend in friends:
            pl.semaphore_signal(barrier, inc=1, device_id=self.device(*friend), device_id_type=MESH)
        pl.semaphore_wait(barrier, len(friends))


class Sender:
    def __init__(self, place, send_sem):
        self.place, self.send_sem, self.pending = place, send_sem, []

    def send(self, source, target, recv_sem, device):
        copy = pltpu.make_async_remote_copy(
            src_ref=source, dst_ref=target, send_sem=self.send_sem.at[len(self.pending)],
            recv_sem=recv_sem, device_id=self.place.device(*device), device_id_type=MESH,
        )
        copy.start()
        self.pending.append(copy)

    def arrived(self, target, recv_sem):
        pltpu.make_async_remote_copy(
            src_ref=target, dst_ref=target, send_sem=self.send_sem.at[0],
            recv_sem=recv_sem, device_id=self.place.device(0, 0, 0, 1), device_id_type=MESH,
        ).wait_recv()

    def drain(self):
        for copy in self.pending:
            copy.wait_send()


def gather_kernel(n_dp, n_fsdp, count, *refs):
    own, full = refs[:count], refs[count : 2 * count]
    send_sem, recv_sem, local_sem = refs[2 * count :]
    place = Place(n_dp, n_fsdp)
    sender = Sender(place, send_sem)
    lines = place.lines
    here = [pltpu.make_async_copy(own[i], full[i].at[place.piece(0, 0, 0, 0)], local_sem.at[i]) for i in range(count)]
    for copy in here:
        copy.start()
    place.greet()

    def forward(piece, device, source=None):
        dd, da, du, dw = piece
        ed, ea, eu, ew = device
        bits = ((du - eu) % 2, (dw - ew) % 2)
        seen = place.slot((dd - ed) % n_dp, (da - ea) % lines, *(bits[::-1] if ed % 2 else bits))
        for i in range(count):
            target = full[i].at[place.piece(*piece)]
            sender.send(target if source is None else source[i], target, recv_sem.at[seen * count + i], device)

    def await_piece(piece):
        for i in range(count):
            sender.arrived(full[i].at[place.piece(*piece)], recv_sem.at[place.slot(*piece) * count + i])

    spread_line = [(0, da, 0, 0) for da in range(1, lines)]
    spread_dp = [(dd, 0, 0, 0) for dd in range(1, n_dp)]
    last = [(0, 0, 0, 1)]
    for device in [(0, 0, 1, 0)] + last + spread_line + spread_dp:
        forward((0, 0, 0, 0), device, own)
    await_piece((0, 0, 1, 0))
    for device in last + spread_line + spread_dp:
        forward((0, 0, 1, 0), device)
    await_piece((0, 0, 0, 1))
    for device in spread_dp:
        forward((0, 0, 0, 1), device)
    for da in sorted(range(1, lines), key=lambda d: min(d, lines - d)):
        for du in range(2):
            await_piece((0, da, du, 0))
            for device in last + spread_dp:
                forward((0, da, du, 0), device)
    for da in range(lines):
        for du in range(2):
            if da or du:
                await_piece((0, da, du, 1))
                for device in spread_dp:
                    forward((0, da, du, 1), device)
    for dd in range(1, n_dp):
        for da in range(lines):
            for du in range(2):
                for dw in range(2):
                    await_piece((dd, da, du, dw))
    for copy in here:
        copy.wait()
    sender.drain()


def gather_pieces(pieces, n_dp, n_fsdp, collective_id):
    count, lines, total = len(pieces), n_fsdp // 4, n_dp * n_fsdp
    sends = (1 + 1 + (lines - 1) * 2 + 1 + (lines - 1) * 2 + n_fsdp * (n_dp - 1)) * count
    return pl.pallas_call(
        partial(gather_kernel, n_dp, n_fsdp, count),
        in_specs=[pl.BlockSpec(memory_space=pltpu.VMEM)] * count,
        out_specs=[pl.BlockSpec(memory_space=pltpu.VMEM)] * count,
        out_shape=[jax.ShapeDtypeStruct((total,) + piece.shape, piece.dtype) for piece in pieces],
        scratch_shapes=[
            pltpu.SemaphoreType.DMA((sends,)),
            pltpu.SemaphoreType.DMA((total * count,)),
            pltpu.SemaphoreType.DMA((count,)),
        ],
        compiler_params=pltpu.CompilerParams(
            collective_id=collective_id, has_side_effects=True, vmem_limit_bytes=40 * 2 ** 20
        ),
        name="gather_pieces",
    )(*pieces)


def scatter_kernel(n_dp, n_fsdp, count, *refs):
    parts, sums = refs[:count], refs[count : 2 * count]
    rest = refs[2 * count :]
    send_sem, recv_sem = rest[0], rest[1]
    got_dp, got_w, got_a, got_u = (rest[2 + k * count : 2 + (k + 1) * count] for k in range(4))
    put_w, put_a, put_u = (rest[2 + k * count : 2 + (k + 1) * count] for k in range(4, 7))
    place = Place(n_dp, n_fsdp)
    sender = Sender(place, send_sem)
    lines = place.lines
    base_w = (n_dp - 1) * n_fsdp
    base_a = base_w + 2 * lines
    base_u = base_a + 2 * (lines - 1)
    place.greet()

    def from_dp(dd, da, du, dw):
        return (dd - 1) * n_fsdp + place.slot(0, da, du, dw)

    def send(source, target, index, base, device):
        for i in range(count):
            sender.send(source(i), target[i].at[index], recv_sem.at[(base + index) * count + i], device)

    def arrived(target, index, base):
        for i in range(count):
            sender.arrived(target[i].at[index], recv_sem.at[(base + index) * count + i])

    order = [(da, du, dw) for dw in (1, 0) for da in list(range(1, lines)) + [0] for du in (1, 0)]
    for da, du, dw in order:
        for dd in range(1, n_dp):
            piece = place.piece(dd, da, *((dw, du) if dd % 2 else (du, dw)))
            send(lambda i: parts[i].at[piece], got_dp, from_dp(n_dp - dd, da, du, dw), 0, (dd, 0, 0, 0))

    def total(i, da, du, dw, extra):
        value = parts[i][place.piece(0, da, du, dw)].astype(F32)
        for dd in range(1, n_dp):
            value += got_dp[i][from_dp(dd, da, du, dw)].astype(F32)
        for ref, index in extra:
            value += ref[i][index].astype(F32)
        return value

    def await_dp(da, du, dw):
        for dd in range(1, n_dp):
            arrived(got_dp, from_dp(dd, da, du, dw), 0)

    for da, du, dw in order:
        await_dp(da, du, dw)
        if dw == 1:
            index = da * 2 + du
            for i in range(count):
                put_w[i][index] = total(i, da, du, 1, []).astype(BF16)
            send(lambda i: put_w[i].at[index], got_w, index, base_w, (0, 0, 0, 1))
    for da in list(range(1, lines)) + [0]:
        for du in (1, 0):
            extra = [(got_w, da * 2 + du)]
            arrived(got_w, da * 2 + du, base_w)
            if da:
                index = (da - 1) * 2 + du
                for i in range(count):
                    put_a[i][index] = total(i, da, du, 0, extra).astype(BF16)
                send(lambda i: put_a[i].at[index], got_a, (lines - da - 1) * 2 + du, base_a, (0, da, 0, 0))
                continue
            for k in range(lines - 1):
                arrived(got_a, k * 2 + du, base_a)
                extra.append((got_a, k * 2 + du))
            if du:
                for i in range(count):
                    put_u[i][0] = total(i, 0, 1, 0, extra).astype(BF16)
                send(lambda i: put_u[i].at[0], got_u, 0, base_u, (0, 0, 1, 0))
            else:
                arrived(got_u, 0, base_u)
                extra.append((got_u, 0))
                for i in range(count):
                    sums[i][...] = total(i, 0, 0, 0, extra)
    sender.drain()


def scatter_sums(parts, n_dp, n_fsdp, collective_id):
    count, lines = len(parts), n_fsdp // 4
    copies = ((n_dp - 1) * n_fsdp + 2 * lines + 2 * (lines - 1) + 1) * count
    sizes = [(n_dp - 1) * n_fsdp, 2 * lines, 2 * (lines - 1), 1, 2 * lines, 2 * (lines - 1), 1]
    buffers = [pltpu.VMEM((size,) + part.shape[1:], BF16) for size in sizes for part in parts]
    return pl.pallas_call(
        partial(scatter_kernel, n_dp, n_fsdp, count),
        in_specs=[pl.BlockSpec(memory_space=pltpu.VMEM)] * count,
        out_specs=[pl.BlockSpec(memory_space=pltpu.VMEM)] * count,
        out_shape=[jax.ShapeDtypeStruct(part.shape[1:], F32) for part in parts],
        scratch_shapes=[pltpu.SemaphoreType.DMA((copies,)), pltpu.SemaphoreType.DMA((copies,))] + buffers,
        compiler_params=pltpu.CompilerParams(
            collective_id=collective_id, has_side_effects=True, vmem_limit_bytes=60 * 2 ** 20
        ),
        name="scatter_sums",
    )(*parts)


D = 768
FF = 3072


epsilon = 1e-06
root_half = 0.7071067811865476
inverse_root_tau = 0.3989422804014327


def normalize_keep(values, gain_vector, shift_vector):
    centred = values - jnp.mean(values, axis=-1, keepdims=True)
    inverse = lax.rsqrt(jnp.mean(centred * centred, axis=-1, keepdims=True) + epsilon)
    scaled = centred * inverse
    return (scaled * gain_vector + shift_vector, scaled, inverse)


def normalize_back(upstream, scaled, inverse, gain_vector):
    weighted = upstream * gain_vector
    centred = weighted - jnp.mean(weighted, axis=-1, keepdims=True)
    result = inverse * (centred - scaled * jnp.mean(weighted * scaled, axis=-1, keepdims=True))
    return (result, jnp.sum(upstream * scaled, axis=0), jnp.sum(upstream, axis=0))


def split_vectors(small_full):
    columns = small_full.astype(jnp.float32)
    pieces = [columns[:, number] for number in range(8)]
    return (pieces, columns[:, 8:].T.reshape(FF))


def per_device(
    tokens,
    cotangent,
    segments,
    padding,
    qkv_weight,
    qkv_moment,
    qkv_average,
    merge_weight,
    merge_moment,
    merge_average,
    expand_weight,
    expand_moment,
    expand_average,
    shrink_weight,
    shrink_moment,
    shrink_average,
    small_params,
    small_moment,
    small_average,
):
    masters = (qkv_weight, merge_weight, expand_weight, shrink_weight, small_params)
    lowered = tuple((master.astype(jnp.bfloat16) for master in masters))
    low_qkv, low_merge, low_expand, low_shrink, low_small = lowered
    axes = ("dp", "fsdp")
    own_rows = qkv_weight.shape[0]
    n_dp, n_fsdp = lax.axis_size("dp"), lax.axis_size("fsdp")
    small_rows = jnp.pad(low_small.reshape(own_rows, -1), ((0, 0), (0, 128 - 8 - FF // D)))
    qkv_full, small_full = gather_pieces([low_qkv, small_rows], n_dp, n_fsdp, 0)
    qkv_full = qkv_full.reshape(D, 3 * D)
    small_full = small_full.reshape(D, 128)[:, : 8 + FF // D]
    second = jnp.concatenate([low_merge, low_expand], axis=1)
    second = lax.all_gather(second, axes, axis=0, tiled=True)
    shrink_full = lax.all_gather(low_shrink, axes, axis=0, tiled=True)
    merge_full, expand_full = second[:, :D], second[:, D:]
    pieces, bias_expand = split_vectors(small_full)
    gain_one, shift_one, bias_query, bias_value, bias_merge, gain_two, shift_two, bias_shrink = (
        pieces
    )
    inputs = tokens.astype(jnp.float32)
    query_mask, key_mask = mask_features(segments, padding, tokens.shape[0])
    norm_one, scaled_one, inverse_one = normalize_keep(inputs, gain_one, shift_one)
    norm_one_low = norm_one.astype(jnp.bfloat16)
    joined = jnp.dot(norm_one_low, qkv_full, preferred_element_type=jnp.float32)
    joined = joined + jnp.concatenate([bias_query, jnp.zeros((D,), jnp.float32), bias_value])
    joined_low = joined.astype(jnp.bfloat16)
    attended_low, attended_wide, logsums = attention_forward(joined_low, query_mask, key_mask)
    middle = (
        inputs + jnp.dot(attended_low, merge_full, preferred_element_type=jnp.float32) + bias_merge
    )
    norm_two, scaled_two, inverse_two = normalize_keep(middle, gain_two, shift_two)
    norm_two_low = norm_two.astype(jnp.bfloat16)
    before = jnp.dot(norm_two_low, expand_full, preferred_element_type=jnp.float32) + bias_expand
    after_low = jax.nn.gelu(before, approximate=False).astype(jnp.bfloat16)
    output = (
        middle + jnp.dot(after_low, shrink_full, preferred_element_type=jnp.float32) + bias_shrink
    )
    activations = output.astype(jnp.bfloat16)
    back_gain_one, back_gain_two = gain_one, gain_two
    outgoing = cotangent.astype(jnp.float32) * padding[:, None].astype(jnp.float32)
    outgoing_low = outgoing.astype(jnp.bfloat16)
    shrink_part = jnp.einsum(
        "sf,sd->fd", after_low, outgoing_low, preferred_element_type=jnp.float32
    )
    shrink_bias_part = jnp.sum(outgoing, axis=0)
    act_grad = jnp.einsum(
        "sd,fd->sf", outgoing_low, shrink_full, preferred_element_type=jnp.float32
    )
    cumulative = 0.5 * (1.0 + lax.erf(before * root_half))
    density = jnp.exp(-0.5 * before * before) * inverse_root_tau
    before_grad = (act_grad * (cumulative + before * density)).astype(jnp.bfloat16)
    expand_part = jnp.einsum(
        "sd,sf->df", norm_two_low, before_grad, preferred_element_type=jnp.float32
    )
    expand_bias_part = jnp.sum(before_grad.astype(jnp.float32), axis=0)
    up_two = jnp.einsum("sf,df->sd", before_grad, expand_full, preferred_element_type=jnp.float32)
    second_back, gain_two_part, shift_two_part = normalize_back(
        up_two, scaled_two, inverse_two, back_gain_two
    )
    middle_grad = outgoing + second_back
    middle_low = middle_grad.astype(jnp.bfloat16)
    merge_part = jnp.einsum(
        "sd,se->de", attended_low, middle_low, preferred_element_type=jnp.float32
    )
    merge_bias_part = jnp.sum(middle_low.astype(jnp.float32), axis=0)
    attended_grad = jnp.einsum(
        "se,de->sd", middle_low, merge_full, preferred_element_type=jnp.float32
    ).astype(jnp.bfloat16)
    query_grads, key_grads, value_grads = attention_backward(
        joined_low, attended_grad, attended_wide, logsums, query_mask, key_mask
    )
    qkv_grad_low = jnp.concatenate([query_grads, key_grads, value_grads], axis=1)
    qkv_part = jnp.einsum(
        "sd,sc->dc", norm_one_low, qkv_grad_low, preferred_element_type=jnp.float32
    )
    column_sums = jnp.sum(qkv_grad_low.astype(jnp.float32), axis=0)
    up_one = jnp.einsum("sc,dc->sd", qkv_grad_low, qkv_full, preferred_element_type=jnp.float32)
    first_back, gain_one_part, shift_one_part = normalize_back(
        up_one, scaled_one, inverse_one, back_gain_one
    )
    input_grad = middle_grad + first_back
    vector_rows = jnp.stack(
        [
            gain_one_part,
            shift_one_part,
            column_sums[:D],
            column_sums[2 * D :],
            merge_bias_part,
            gain_two_part,
            shift_two_part,
            shrink_bias_part,
        ]
    )
    all_rows = jnp.concatenate([vector_rows, expand_bias_part.reshape(FF // D, D)], axis=0)
    small_part = all_rows.T
    wide_part = jnp.concatenate([merge_part, expand_part], axis=1).astype(BF16)
    shrink_sum = lax.psum_scatter(shrink_part.astype(BF16), axes, scatter_dimension=0, tiled=True)
    wide_sum = lax.psum_scatter(wide_part, axes, scatter_dimension=0, tiled=True).astype(F32)
    small_part = jnp.pad(small_part, ((0, 0), (0, 128 - 8 - FF // D)))
    last_parts = [part.astype(BF16).reshape(n_dp * n_fsdp, own_rows, -1) for part in (qkv_part, small_part)]
    qkv_sum, small_sum = scatter_sums(last_parts, n_dp, n_fsdp, 1)
    summed = (
        qkv_sum,
        wide_sum[:, :D],
        wide_sum[:, D:],
        shrink_sum.astype(F32),
        small_sum[:, : 8 + FF // D].reshape(-1),
    )
    rate_scale = (tokens.shape[0] * lax.axis_size("dp") * lax.axis_size("fsdp")) ** (-0.5)
    rates = (
        0.04 * rate_scale,
        4.0 * rate_scale,
        0.08 * rate_scale,
        0.02 * rate_scale,
        0.07 * rate_scale,
    )
    moments = (qkv_moment, merge_moment, expand_moment, shrink_moment, small_moment)
    averages = (qkv_average, merge_average, expand_average, shrink_average, small_average)
    results = [activations, input_grad]
    for master, gradient, moment, average, step_rate in zip(
        masters, summed, moments, averages, rates
    ):
        fresh_moment = 0.5 * moment + gradient
        updated = master - step_rate * (gradient + 0.5 * fresh_moment)
        results.extend(
            [
                gradient,
                fresh_moment,
                updated,
                0.5 * average + 0.5 * updated,
                updated.astype(jnp.bfloat16),
            ]
        )
    return tuple(results)


def solution(mesh):
    placed = (
        P(("dp", "fsdp"), None),
        P(("dp", "fsdp"), None),
        P(("dp", "fsdp")),
        P(("dp", "fsdp")),
        P(("dp", "fsdp"), None),
        P(("dp", "fsdp"), None),
        P(("dp", "fsdp"), None),
        P(("dp", "fsdp"), None),
        P(("dp", "fsdp"), None),
        P(("dp", "fsdp"), None),
        P(("dp", "fsdp"), None),
        P(("dp", "fsdp"), None),
        P(("dp", "fsdp"), None),
        P(("dp", "fsdp"), None),
        P(("dp", "fsdp"), None),
        P(("dp", "fsdp"), None),
        P(("dp", "fsdp")),
        P(("dp", "fsdp")),
        P(("dp", "fsdp")),
    )
    return jax.shard_map(
        per_device,
        mesh=mesh,
        in_specs=placed,
        out_specs=(
            P(("dp", "fsdp"), None),
            P(("dp", "fsdp"), None),
            P(("dp", "fsdp"), None),
            P(("dp", "fsdp"), None),
            P(("dp", "fsdp"), None),
            P(("dp", "fsdp"), None),
            P(("dp", "fsdp"), None),
            P(("dp", "fsdp"), None),
            P(("dp", "fsdp"), None),
            P(("dp", "fsdp"), None),
            P(("dp", "fsdp"), None),
            P(("dp", "fsdp"), None),
            P(("dp", "fsdp"), None),
            P(("dp", "fsdp"), None),
            P(("dp", "fsdp"), None),
            P(("dp", "fsdp"), None),
            P(("dp", "fsdp"), None),
            P(("dp", "fsdp"), None),
            P(("dp", "fsdp"), None),
            P(("dp", "fsdp"), None),
            P(("dp", "fsdp"), None),
            P(("dp", "fsdp"), None),
            P(("dp", "fsdp")),
            P(("dp", "fsdp")),
            P(("dp", "fsdp")),
            P(("dp", "fsdp")),
            P(("dp", "fsdp")),
        ),
        check_vma=False,
    )
```

```python
from functools import partial
import jax, jax.numpy as jnp
from jax import lax
from jax.sharding import PartitionSpec as P
from jax.experimental import pallas as pl
from jax.experimental.pallas import tpu as pltpu

HEAD_DIM = 64
BIG = 2.0 ** 100
F32 = jnp.float32
BF16 = jnp.bfloat16


def round_up(n, m):
    return (n + m - 1) // m * m


def mask_features(segments, padding, slots):
    wide = round_up(slots, 256)
    group = segments * 2 + padding
    group = jnp.concatenate([group, jnp.full((wide - slots,), 4, jnp.int32)])[:, None]
    lane = lax.broadcasted_iota(jnp.int32, (wide, 128), 1) % HEAD_DIM
    same = group == lane
    query_side = jnp.where((lane < 5) & ~same, -BIG, 0.0).astype(BF16)
    key_side = jnp.where(same | ((lane >= 5) & (lane < 8)), 1.0, 0.0).astype(BF16)
    return query_side, key_side


def dot_nt(a, b):
    return lax.dot_general(a, b, (((1,), (1,)), ((), ())), preferred_element_type=F32)


def dot_nn(a, b):
    return lax.dot_general(a, b, (((1,), (0,)), ((), ())), preferred_element_type=F32)


def dot_tn(a, b):
    return lax.dot_general(a, b, (((0,), (0,)), ((), ())), preferred_element_type=F32)


def fill(target, value, features, keep_low, slots):
    wide = target.shape[0]
    start = slots // 16 * 16
    low_half = lax.broadcasted_iota(jnp.int32, (wide - start, 128), 1) < HEAD_DIM
    tail = features[start:wide, :] if features is not None else jnp.ones((wide - start, 128), BF16)
    target[start:wide, :] = jnp.where(low_half == keep_low, jnp.zeros_like(tail), tail)
    target[0:slots, :] = value


def forward_kernel(slots, block, q_ref, k_ref, v_ref, fq_ref, fk_ref,
                   low_ref, wide_ref, lse_ref, qa, qb, ka, kb, va, vb, out, lse):
    low_half = lax.broadcasted_iota(jnp.int32, (slots, 128), 1) < HEAD_DIM
    q = q_ref[...] * 0.125
    fq = fq_ref[0:slots, :]
    fk = fk_ref[0:slots, :]
    fill(qa, jnp.where(low_half, q, fq), fq_ref, True, slots)
    fill(qb, jnp.where(low_half, fq, q), fq_ref, False, slots)
    k = k_ref[...]
    fill(ka, jnp.where(low_half, k, fk), fk_ref, True, slots)
    fill(kb, jnp.where(low_half, fk, k), fk_ref, False, slots)
    v = v_ref[...]
    one = jnp.ones_like(v)
    fill(va, jnp.where(low_half, v, one), None, True, slots)
    fill(vb, jnp.where(low_half, one, v), None, False, slots)
    half = lax.broadcasted_iota(jnp.int32, (block, 128), 1) < HEAD_DIM

    def head(qx, kx, vx, rows):
        scores = dot_nt(qx[rows, :], kx[...])
        top = jnp.max(scores, axis=1, keepdims=True)
        weights = jnp.exp(scores - top).astype(BF16)
        return dot_nn(weights, vx[...]), top

    def step(number, carry):
        rows = pl.ds(pl.multiple_of(number * block, 16), block)
        raw_a, top_a = head(qa, ka, va, rows)
        raw_b, top_b = head(qb, kb, vb, rows)
        sums = jnp.where(half, raw_b, raw_a)
        lse[rows, :] = jnp.where(half, top_b, top_a) + jnp.log(sums)
        out[rows, :] = jnp.where(half, raw_a, raw_b) / pltpu.roll(sums, HEAD_DIM, 1)
        return carry

    lax.fori_loop(0, out.shape[0] // block, step, 0)
    attended = out[0:slots, :]
    low_ref[...] = attended.astype(BF16)
    wide_ref[...] = attended
    lse_ref[...] = lse[0:slots, :]


def column(shift, slots):
    return pl.BlockSpec((slots, 128), lambda p, s=shift: (0, s + p))


def attention_forward(qkv, fq, fk, block=240):
    slots = qkv.shape[0]
    pairs = qkv.shape[1] // 384
    wide = fq.shape[0]
    rows = round_up(slots, block)
    whole = pl.BlockSpec((wide, 128), lambda p: (0, 0))
    width = pairs * 128
    return pl.pallas_call(
        partial(forward_kernel, slots, block),
        grid=(pairs,),
        in_specs=[column(0, slots), column(pairs, slots), column(2 * pairs, slots), whole, whole],
        out_specs=[column(0, slots)] * 3,
        out_shape=[
            jax.ShapeDtypeStruct((slots, width), BF16),
            jax.ShapeDtypeStruct((slots, width), F32),
            jax.ShapeDtypeStruct((slots, width), F32),
        ],
        scratch_shapes=[pltpu.VMEM((wide, 128), BF16)] * 6 + [pltpu.VMEM((rows, 128), F32)] * 2,
        compiler_params=pltpu.CompilerParams(vmem_limit_bytes=50 * 2 ** 20),
        name="attention_forward",
    )(qkv, qkv, qkv, fq, fk)


def thirds(value):
    high = value.astype(BF16)
    rest = value - high.astype(F32)
    mid = rest.astype(BF16)
    return high, mid, (rest - mid.astype(F32)).astype(BF16)


def backward_kernel(slots, block, q_ref, k_ref, v_ref, g_ref, wide_ref, lse_ref, fq_ref, fk_ref,
                    dq_ref, dk_ref, dv_ref, qa, qb, ka, kb, va, vb, ga, gb, dqa, dqb, dk, dv):
    lane = lax.broadcasted_iota(jnp.int32, (slots, 128), 1)
    low_half = lane < HEAD_DIM
    spot = lane % HEAD_DIM
    q = q_ref[...] * 0.125
    fk = fk_ref[0:slots, :]
    high, mid, low = thirds(-lse_ref[...])
    fq = jnp.where(spot == 5, high, jnp.where(spot == 6, mid, jnp.where(spot == 7, low, fq_ref[0:slots, :])))
    fill(qa, jnp.where(low_half, q, fq), fq_ref, True, slots)
    fill(qb, jnp.where(low_half, fq, q), fq_ref, False, slots)
    k = k_ref[...]
    fill(ka, jnp.where(low_half, k, fk), fk_ref, True, slots)
    fill(kb, jnp.where(low_half, fk, k), fk_ref, False, slots)
    v = v_ref[...]
    one = jnp.ones_like(v)
    fill(va, jnp.where(low_half, v, one), None, True, slots)
    fill(vb, jnp.where(low_half, one, v), None, False, slots)
    g = g_ref[...]
    product = g.astype(F32) * wide_ref[...]
    delta_a = jnp.sum(jnp.where(low_half, product, 0.0), axis=1, keepdims=True)
    delta_b = jnp.sum(jnp.where(low_half, 0.0, product), axis=1, keepdims=True)
    high, mid, low = thirds(-jnp.where(low_half, delta_b, delta_a))
    zero = jnp.zeros_like(g)
    fg = jnp.where(spot == 0, high, jnp.where(spot == 1, mid, jnp.where(spot == 2, low, zero)))
    ga[...] = jnp.zeros_like(ga)
    gb[...] = jnp.zeros_like(gb)
    ga[0:slots, :] = jnp.where(low_half, g, fg)
    gb[0:slots, :] = jnp.where(low_half, fg, g)
    dqa[...] = jnp.zeros_like(dqa)
    dqb[...] = jnp.zeros_like(dqb)
    half = lax.broadcasted_iota(jnp.int32, (block, 128), 1) < HEAD_DIM

    def head(qx, kx, vx, gx, dqx, rows):
        keys = kx[rows, :]
        probs = jnp.exp(dot_nt(keys, qx[...]))
        value_grad = dot_nn(probs.astype(BF16), gx[...])
        score_grad = (probs * dot_nt(vx[rows, :], gx[...])).astype(BF16)
        key_grad = dot_nn(score_grad, qx[...])
        dqx[...] += dot_tn(score_grad, keys)
        return key_grad, value_grad

    def step(number, carry):
        rows = pl.ds(pl.multiple_of(number * block, 16), block)
        key_a, value_a = head(qa, ka, va, ga, dqa, rows)
        key_b, value_b = head(qb, kb, vb, gb, dqb, rows)
        dk[rows, :] = jnp.where(half, key_a, key_b)
        dv[rows, :] = jnp.where(half, value_a, value_b)
        return carry

    lax.fori_loop(0, dk.shape[0] // block, step, 0)
    dq_ref[...] = (jnp.where(low_half, dqa[0:slots, :], dqb[0:slots, :]) * 0.125).astype(BF16)
    dk_ref[...] = dk[0:slots, :].astype(BF16)
    dv_ref[...] = dv[0:slots, :].astype(BF16)


def attention_backward(qkv, upstream, wide_out, lse, fq, fk, block=240):
    slots = qkv.shape[0]
    pairs = qkv.shape[1] // 384
    wide = fq.shape[0]
    rows = round_up(slots, block)
    whole = pl.BlockSpec((wide, 128), lambda p: (0, 0))
    width = pairs * 128
    return pl.pallas_call(
        partial(backward_kernel, slots, block),
        grid=(pairs,),
        in_specs=[column(0, slots), column(pairs, slots), column(2 * pairs, slots),
                  column(0, slots), column(0, slots), column(0, slots), whole, whole],
        out_specs=[column(0, slots)] * 3,
        out_shape=[jax.ShapeDtypeStruct((slots, width), BF16)] * 3,
        scratch_shapes=[pltpu.VMEM((wide, 128), BF16)] * 8
        + [pltpu.VMEM((wide, 128), F32)] * 2 + [pltpu.VMEM((rows, 128), F32)] * 2,
        compiler_params=pltpu.CompilerParams(vmem_limit_bytes=60 * 2 ** 20),
        name="attention_backward",
    )(qkv, qkv, qkv, upstream, wide_out, lse, fq, fk)


root_half = 0.7071067811865476
inverse_root_tau = 0.3989422804014327


def expand_kernel(chunk, x_ref, w_ref, b_ref, after_ref, slope_ref):
    x = x_ref[...]

    def step(number, carry):
        cols = pl.ds(pl.multiple_of(number * chunk, 128), chunk)
        before = dot_nn(x, w_ref[:, cols]) + b_ref[:, cols]
        cumulative = 0.5 * (1.0 + lax.erf(before * root_half))
        density = jnp.exp(-0.5 * before * before) * inverse_root_tau
        after_ref[:, cols] = (before * cumulative).astype(BF16)
        slope_ref[:, cols] = (cumulative + before * density).astype(BF16)
        return carry

    lax.fori_loop(0, w_ref.shape[1] // chunk, step, 0)


def expand_forward(x, weight, bias, block=240, chunk=768):
    slots, inner = x.shape
    hidden = weight.shape[1]
    return pl.pallas_call(
        partial(expand_kernel, chunk),
        grid=(round_up(slots, block) // block,),
        in_specs=[
            pl.BlockSpec((block, inner), lambda r: (r, 0)),
            pl.BlockSpec((inner, hidden), lambda r: (0, 0)),
            pl.BlockSpec((1, hidden), lambda r: (0, 0)),
        ],
        out_specs=[pl.BlockSpec((block, hidden), lambda r: (r, 0))] * 2,
        out_shape=[jax.ShapeDtypeStruct((slots, hidden), BF16)] * 2,
        compiler_params=pltpu.CompilerParams(vmem_limit_bytes=40 * 2 ** 20),
        name="expand_forward",
    )(x, weight, bias.reshape(1, -1))


MESH = pl.DeviceIdType.MESH


class Place:
    def __init__(self, n_dp, n_fsdp):
        self.n_dp, self.n_fsdp, self.lines = n_dp, n_fsdp, n_fsdp // 4
        self.dp, at = lax.axis_index("dp"), lax.axis_index("fsdp")
        core = self.dp % 2
        self.stride_u, self.stride_w = 2 - core, 1 + core
        high, low = (at // 2) % 2, at % 2
        self.a = at // 4
        self.u = high * (1 - core) + low * core
        self.w = low * (1 - core) + high * core

    def fsdp_of(self, da, du, dw):
        a, u, w = (self.a + da) % self.lines, (self.u + du) % 2, (self.w + dw) % 2
        return a * 4 + u * self.stride_u + w * self.stride_w

    def dp_of(self, dd):
        return (self.dp + dd) % self.n_dp

    def piece(self, dd, da, du, dw):
        return self.dp_of(dd) * self.n_fsdp + self.fsdp_of(da, du, dw)

    def device(self, dd, da, du, dw):
        return (self.dp_of(dd), self.fsdp_of(da, du, dw))

    def slot(self, dd, da, du, dw):
        return ((dd * self.lines + da) * 2 + du) * 2 + dw

    def greet(self):
        barrier = pltpu.get_barrier_semaphore()
        friends = [(0, 0, 1, 0), (0, 0, 0, 1)]
        friends += [(0, da, 0, 0) for da in range(1, self.lines)]
        friends += [(dd, 0, 0, 0) for dd in range(1, self.n_dp)]
        for friend in friends:
            pl.semaphore_signal(barrier, inc=1, device_id=self.device(*friend), device_id_type=MESH)
        pl.semaphore_wait(barrier, len(friends))


class Sender:
    def __init__(self, place, send_sem):
        self.place, self.send_sem, self.pending = place, send_sem, []

    def send(self, source, target, recv_sem, device):
        copy = pltpu.make_async_remote_copy(
            src_ref=source, dst_ref=target, send_sem=self.send_sem.at[len(self.pending)],
            recv_sem=recv_sem, device_id=self.place.device(*device), device_id_type=MESH,
        )
        copy.start()
        self.pending.append(copy)

    def arrived(self, target, recv_sem):
        pltpu.make_async_remote_copy(
            src_ref=target, dst_ref=target, send_sem=self.send_sem.at[0],
            recv_sem=recv_sem, device_id=self.place.device(0, 0, 0, 1), device_id_type=MESH,
        ).wait_recv()

    def drain(self):
        for copy in self.pending:
            copy.wait_send()


def gather_kernel(n_dp, n_fsdp, count, *refs):
    own, full = refs[:count], refs[count : 2 * count]
    send_sem, recv_sem, local_sem = refs[2 * count :]
    place = Place(n_dp, n_fsdp)
    sender = Sender(place, send_sem)
    lines = place.lines
    here = [pltpu.make_async_copy(own[i], full[i].at[place.piece(0, 0, 0, 0)], local_sem.at[i]) for i in range(count)]
    for copy in here:
        copy.start()
    place.greet()

    def forward(piece, device, source=None):
        dd, da, du, dw = piece
        ed, ea, eu, ew = device
        bits = ((du - eu) % 2, (dw - ew) % 2)
        seen = place.slot((dd - ed) % n_dp, (da - ea) % lines, *(bits[::-1] if ed % 2 else bits))
        for i in range(count):
            target = full[i].at[place.piece(*piece)]
            sender.send(target if source is None else source[i], target, recv_sem.at[seen * count + i], device)

    def await_piece(piece):
        for i in range(count):
            sender.arrived(full[i].at[place.piece(*piece)], recv_sem.at[place.slot(*piece) * count + i])

    spread_line = [(0, da, 0, 0) for da in range(1, lines)]
    spread_dp = [(dd, 0, 0, 0) for dd in range(1, n_dp)]
    last = [(0, 0, 0, 1)]
    for device in [(0, 0, 1, 0)] + last + spread_line + spread_dp:
        forward((0, 0, 0, 0), device, own)
    await_piece((0, 0, 1, 0))
    for device in last + spread_line + spread_dp:
        forward((0, 0, 1, 0), device)
    await_piece((0, 0, 0, 1))
    for device in spread_dp:
        forward((0, 0, 0, 1), device)
    for da in sorted(range(1, lines), key=lambda d: min(d, lines - d)):
        for du in range(2):
            await_piece((0, da, du, 0))
            for device in last + spread_dp:
                forward((0, da, du, 0), device)
    for da in range(lines):
        for du in range(2):
            if da or du:
                await_piece((0, da, du, 1))
                for device in spread_dp:
                    forward((0, da, du, 1), device)
    for dd in range(1, n_dp):
        for da in range(lines):
            for du in range(2):
                for dw in range(2):
                    await_piece((dd, da, du, dw))
    for copy in here:
        copy.wait()
    sender.drain()


def gather_pieces(pieces, n_dp, n_fsdp, collective_id):
    count, lines, total = len(pieces), n_fsdp // 4, n_dp * n_fsdp
    sends = (1 + 1 + (lines - 1) * 2 + 1 + (lines - 1) * 2 + n_fsdp * (n_dp - 1)) * count
    return pl.pallas_call(
        partial(gather_kernel, n_dp, n_fsdp, count),
        in_specs=[pl.BlockSpec(memory_space=pltpu.VMEM)] * count,
        out_specs=[pl.BlockSpec(memory_space=pltpu.VMEM)] * count,
        out_shape=[jax.ShapeDtypeStruct((total,) + piece.shape, piece.dtype) for piece in pieces],
        scratch_shapes=[
            pltpu.SemaphoreType.DMA((sends,)),
            pltpu.SemaphoreType.DMA((total * count,)),
            pltpu.SemaphoreType.DMA((count,)),
        ],
        compiler_params=pltpu.CompilerParams(
            collective_id=collective_id, has_side_effects=True, vmem_limit_bytes=40 * 2 ** 20
        ),
        name="gather_pieces",
    )(*pieces)


def scatter_kernel(n_dp, n_fsdp, count, *refs):
    parts, sums = refs[:count], refs[count : 2 * count]
    rest = refs[2 * count :]
    send_sem, recv_sem = rest[0], rest[1]
    got_dp, got_w, got_a, got_u = (rest[2 + k * count : 2 + (k + 1) * count] for k in range(4))
    put_w, put_a, put_u = (rest[2 + k * count : 2 + (k + 1) * count] for k in range(4, 7))
    place = Place(n_dp, n_fsdp)
    sender = Sender(place, send_sem)
    lines = place.lines
    base_w = (n_dp - 1) * n_fsdp
    base_a = base_w + 2 * lines
    base_u = base_a + 2 * (lines - 1)
    place.greet()

    def from_dp(dd, da, du, dw):
        return (dd - 1) * n_fsdp + place.slot(0, da, du, dw)

    def send(source, target, index, base, device):
        for i in range(count):
            sender.send(source(i), target[i].at[index], recv_sem.at[(base + index) * count + i], device)

    def arrived(target, index, base):
        for i in range(count):
            sender.arrived(target[i].at[index], recv_sem.at[(base + index) * count + i])

    order = [(da, du, dw) for dw in (1, 0) for da in list(range(1, lines)) + [0] for du in (1, 0)]
    for da, du, dw in order:
        for dd in range(1, n_dp):
            piece = place.piece(dd, da, *((dw, du) if dd % 2 else (du, dw)))
            send(lambda i: parts[i].at[piece], got_dp, from_dp(n_dp - dd, da, du, dw), 0, (dd, 0, 0, 0))

    def total(i, da, du, dw, extra):
        value = parts[i][place.piece(0, da, du, dw)].astype(F32)
        for dd in range(1, n_dp):
            value += got_dp[i][from_dp(dd, da, du, dw)].astype(F32)
        for ref, index in extra:
            value += ref[i][index].astype(F32)
        return value

    def await_dp(da, du, dw):
        for dd in range(1, n_dp):
            arrived(got_dp, from_dp(dd, da, du, dw), 0)

    for da, du, dw in order:
        await_dp(da, du, dw)
        if dw == 1:
            index = da * 2 + du
            for i in range(count):
                put_w[i][index] = total(i, da, du, 1, []).astype(BF16)
            send(lambda i: put_w[i].at[index], got_w, index, base_w, (0, 0, 0, 1))
    for da in list(range(1, lines)) + [0]:
        for du in (1, 0):
            extra = [(got_w, da * 2 + du)]
            arrived(got_w, da * 2 + du, base_w)
            if da:
                index = (da - 1) * 2 + du
                for i in range(count):
                    put_a[i][index] = total(i, da, du, 0, extra).astype(BF16)
                send(lambda i: put_a[i].at[index], got_a, (lines - da - 1) * 2 + du, base_a, (0, da, 0, 0))
                continue
            for k in range(lines - 1):
                arrived(got_a, k * 2 + du, base_a)
                extra.append((got_a, k * 2 + du))
            if du:
                for i in range(count):
                    put_u[i][0] = total(i, 0, 1, 0, extra).astype(BF16)
                send(lambda i: put_u[i].at[0], got_u, 0, base_u, (0, 0, 1, 0))
            else:
                arrived(got_u, 0, base_u)
                extra.append((got_u, 0))
                for i in range(count):
                    sums[i][...] = total(i, 0, 0, 0, extra)
    sender.drain()


def scatter_sums(parts, n_dp, n_fsdp, collective_id):
    count, lines = len(parts), n_fsdp // 4
    copies = ((n_dp - 1) * n_fsdp + 2 * lines + 2 * (lines - 1) + 1) * count
    sizes = [(n_dp - 1) * n_fsdp, 2 * lines, 2 * (lines - 1), 1, 2 * lines, 2 * (lines - 1), 1]
    buffers = [pltpu.VMEM((size,) + part.shape[1:], BF16) for size in sizes for part in parts]
    return pl.pallas_call(
        partial(scatter_kernel, n_dp, n_fsdp, count),
        in_specs=[pl.BlockSpec(memory_space=pltpu.VMEM)] * count,
        out_specs=[pl.BlockSpec(memory_space=pltpu.VMEM)] * count,
        out_shape=[jax.ShapeDtypeStruct(part.shape[1:], F32) for part in parts],
        scratch_shapes=[pltpu.SemaphoreType.DMA((copies,)), pltpu.SemaphoreType.DMA((copies,))] + buffers,
        compiler_params=pltpu.CompilerParams(
            collective_id=collective_id, has_side_effects=True, vmem_limit_bytes=60 * 2 ** 20
        ),
        name="scatter_sums",
    )(*parts)


D = 768
FF = 3072


epsilon = 1e-06


def normalize_keep(values, gain_vector, shift_vector):
    centred = values - jnp.mean(values, axis=-1, keepdims=True)
    inverse = lax.rsqrt(jnp.mean(centred * centred, axis=-1, keepdims=True) + epsilon)
    scaled = centred * inverse
    return (scaled * gain_vector + shift_vector, scaled, inverse)


def normalize_back(upstream, scaled, inverse, gain_vector):
    weighted = upstream * gain_vector
    centred = weighted - jnp.mean(weighted, axis=-1, keepdims=True)
    result = inverse * (centred - scaled * jnp.mean(weighted * scaled, axis=-1, keepdims=True))
    return (result, jnp.sum(upstream * scaled, axis=0), jnp.sum(upstream, axis=0))


def split_vectors(small_full):
    columns = small_full.astype(jnp.float32)
    pieces = [columns[:, number] for number in range(8)]
    return (pieces, columns[:, 8:].T.reshape(FF))


def per_device(
    tokens,
    cotangent,
    segments,
    padding,
    qkv_weight,
    qkv_moment,
    qkv_average,
    merge_weight,
    merge_moment,
    merge_average,
    expand_weight,
    expand_moment,
    expand_average,
    shrink_weight,
    shrink_moment,
    shrink_average,
    small_params,
    small_moment,
    small_average,
):
    masters = (qkv_weight, merge_weight, expand_weight, shrink_weight, small_params)
    lowered = tuple((master.astype(jnp.bfloat16) for master in masters))
    low_qkv, low_merge, low_expand, low_shrink, low_small = lowered
    axes = ("dp", "fsdp")
    own_rows = qkv_weight.shape[0]
    n_dp, n_fsdp = lax.axis_size("dp"), lax.axis_size("fsdp")
    small_rows = jnp.pad(low_small.reshape(own_rows, -1), ((0, 0), (0, 128 - 8 - FF // D)))
    qkv_full, small_full = gather_pieces([low_qkv, small_rows], n_dp, n_fsdp, 0)
    qkv_full = qkv_full.reshape(D, 3 * D)
    small_full = small_full.reshape(D, 128)[:, : 8 + FF // D]
    second = jnp.concatenate([low_merge, low_expand], axis=1)
    second = lax.all_gather(second, axes, axis=0, tiled=True)
    shrink_full = lax.all_gather(low_shrink, axes, axis=0, tiled=True)
    merge_full, expand_full = second[:, :D], second[:, D:]
    pieces, bias_expand = split_vectors(small_full)
    gain_one, shift_one, bias_query, bias_value, bias_merge, gain_two, shift_two, bias_shrink = (
        pieces
    )
    inputs = tokens.astype(jnp.float32)
    query_mask, key_mask = mask_features(segments, padding, tokens.shape[0])
    norm_one, scaled_one, inverse_one = normalize_keep(inputs, gain_one, shift_one)
    norm_one_low = norm_one.astype(jnp.bfloat16)
    joined = jnp.dot(norm_one_low, qkv_full, preferred_element_type=jnp.float32)
    joined = joined + jnp.concatenate([bias_query, jnp.zeros((D,), jnp.float32), bias_value])
    joined_low = joined.astype(jnp.bfloat16)
    attended_low, attended_wide, logsums = attention_forward(joined_low, query_mask, key_mask)
    middle = (
        inputs + jnp.dot(attended_low, merge_full, preferred_element_type=jnp.float32) + bias_merge
    )
    norm_two, scaled_two, inverse_two = normalize_keep(middle, gain_two, shift_two)
    norm_two_low = norm_two.astype(jnp.bfloat16)
    after_low, slope = expand_forward(norm_two_low, expand_full, bias_expand)
    output = (
        middle + jnp.dot(after_low, shrink_full, preferred_element_type=jnp.float32) + bias_shrink
    )
    activations = output.astype(jnp.bfloat16)
    back_gain_one, back_gain_two = gain_one, gain_two
    outgoing = cotangent.astype(jnp.float32) * padding[:, None].astype(jnp.float32)
    outgoing_low = outgoing.astype(jnp.bfloat16)
    shrink_part = jnp.einsum(
        "sf,sd->fd", after_low, outgoing_low, preferred_element_type=jnp.float32
    )
    shrink_bias_part = jnp.sum(outgoing, axis=0)
    shrink_low, shrink_full = lax.optimization_barrier((shrink_part.astype(BF16), shrink_full))
    act_grad = jnp.einsum(
        "sd,fd->sf", outgoing_low, shrink_full, preferred_element_type=jnp.float32
    )
    before_grad = (act_grad * slope.astype(F32)).astype(BF16)
    expand_part = jnp.einsum(
        "sd,sf->df", norm_two_low, before_grad, preferred_element_type=jnp.float32
    )
    expand_bias_part = jnp.sum(before_grad.astype(jnp.float32), axis=0)
    up_two = jnp.einsum("sf,df->sd", before_grad, expand_full, preferred_element_type=jnp.float32)
    second_back, gain_two_part, shift_two_part = normalize_back(
        up_two, scaled_two, inverse_two, back_gain_two
    )
    middle_grad = outgoing + second_back
    middle_low = middle_grad.astype(jnp.bfloat16)
    merge_part = jnp.einsum(
        "sd,se->de", attended_low, middle_low, preferred_element_type=jnp.float32
    )
    merge_bias_part = jnp.sum(middle_low.astype(jnp.float32), axis=0)
    attended_grad = jnp.einsum(
        "se,de->sd", middle_low, merge_full, preferred_element_type=jnp.float32
    ).astype(jnp.bfloat16)
    query_grads, key_grads, value_grads = attention_backward(
        joined_low, attended_grad, attended_wide, logsums, query_mask, key_mask
    )
    qkv_grad_low = jnp.concatenate([query_grads, key_grads, value_grads], axis=1)
    qkv_part = jnp.einsum(
        "sd,sc->dc", norm_one_low, qkv_grad_low, preferred_element_type=jnp.float32
    )
    column_sums = jnp.sum(qkv_grad_low.astype(jnp.float32), axis=0)
    up_one = jnp.einsum("sc,dc->sd", qkv_grad_low, qkv_full, preferred_element_type=jnp.float32)
    first_back, gain_one_part, shift_one_part = normalize_back(
        up_one, scaled_one, inverse_one, back_gain_one
    )
    input_grad = middle_grad + first_back
    vector_rows = jnp.stack(
        [
            gain_one_part,
            shift_one_part,
            column_sums[:D],
            column_sums[2 * D :],
            merge_bias_part,
            gain_two_part,
            shift_two_part,
            shrink_bias_part,
        ]
    )
    all_rows = jnp.concatenate([vector_rows, expand_bias_part.reshape(FF // D, D)], axis=0)
    small_part = all_rows.T
    wide_part = jnp.concatenate([merge_part, expand_part], axis=1).astype(BF16)
    shrink_sum = lax.psum_scatter(shrink_low, axes, scatter_dimension=0, tiled=True)
    wide_sum = lax.psum_scatter(wide_part, axes, scatter_dimension=0, tiled=True).astype(F32)
    small_part = jnp.pad(small_part, ((0, 0), (0, 128 - 8 - FF // D)))
    last_parts = [part.astype(BF16).reshape(n_dp * n_fsdp, own_rows, -1) for part in (qkv_part, small_part)]
    qkv_sum, small_sum = scatter_sums(last_parts, n_dp, n_fsdp, 1)
    summed = (
        qkv_sum,
        wide_sum[:, :D],
        wide_sum[:, D:],
        shrink_sum.astype(F32),
        small_sum[:, : 8 + FF // D].reshape(-1),
    )
    rate_scale = (tokens.shape[0] * lax.axis_size("dp") * lax.axis_size("fsdp")) ** (-0.5)
    rates = (
        0.04 * rate_scale,
        4.0 * rate_scale,
        0.08 * rate_scale,
        0.02 * rate_scale,
        0.07 * rate_scale,
    )
    moments = (qkv_moment, merge_moment, expand_moment, shrink_moment, small_moment)
    averages = (qkv_average, merge_average, expand_average, shrink_average, small_average)
    results = [activations, input_grad]
    for master, gradient, moment, average, step_rate in zip(
        masters, summed, moments, averages, rates
    ):
        fresh_moment = 0.5 * moment + gradient
        updated = master - step_rate * (gradient + 0.5 * fresh_moment)
        results.extend(
            [
                gradient,
                fresh_moment,
                updated,
                0.5 * average + 0.5 * updated,
                updated.astype(jnp.bfloat16),
            ]
        )
    return tuple(results)


def solution(mesh):
    placed = (
        P(("dp", "fsdp"), None),
        P(("dp", "fsdp"), None),
        P(("dp", "fsdp")),
        P(("dp", "fsdp")),
        P(("dp", "fsdp"), None),
        P(("dp", "fsdp"), None),
        P(("dp", "fsdp"), None),
        P(("dp", "fsdp"), None),
        P(("dp", "fsdp"), None),
        P(("dp", "fsdp"), None),
        P(("dp", "fsdp"), None),
        P(("dp", "fsdp"), None),
        P(("dp", "fsdp"), None),
        P(("dp", "fsdp"), None),
        P(("dp", "fsdp"), None),
        P(("dp", "fsdp"), None),
        P(("dp", "fsdp")),
        P(("dp", "fsdp")),
        P(("dp", "fsdp")),
    )
    return jax.shard_map(
        per_device,
        mesh=mesh,
        in_specs=placed,
        out_specs=(
            P(("dp", "fsdp"), None),
            P(("dp", "fsdp"), None),
            P(("dp", "fsdp"), None),
            P(("dp", "fsdp"), None),
            P(("dp", "fsdp"), None),
            P(("dp", "fsdp"), None),
            P(("dp", "fsdp"), None),
            P(("dp", "fsdp"), None),
            P(("dp", "fsdp"), None),
            P(("dp", "fsdp"), None),
            P(("dp", "fsdp"), None),
            P(("dp", "fsdp"), None),
            P(("dp", "fsdp"), None),
            P(("dp", "fsdp"), None),
            P(("dp", "fsdp"), None),
            P(("dp", "fsdp"), None),
            P(("dp", "fsdp"), None),
            P(("dp", "fsdp"), None),
            P(("dp", "fsdp"), None),
            P(("dp", "fsdp"), None),
            P(("dp", "fsdp"), None),
            P(("dp", "fsdp"), None),
            P(("dp", "fsdp")),
            P(("dp", "fsdp")),
            P(("dp", "fsdp")),
            P(("dp", "fsdp")),
            P(("dp", "fsdp")),
        ),
        check_vma=False,
    )
```

```python
from functools import partial
import jax, jax.numpy as jnp
from jax import lax
from jax.sharding import PartitionSpec as P
from jax.experimental import pallas as pl
from jax.experimental.pallas import tpu as pltpu

HEAD_DIM = 64
BIG = 2.0 ** 100
F32 = jnp.float32
BF16 = jnp.bfloat16


def round_up(n, m):
    return (n + m - 1) // m * m


def mask_features(segments, padding, slots):
    wide = round_up(slots, 256)
    group = segments * 2 + padding
    group = jnp.concatenate([group, jnp.full((wide - slots,), 4, jnp.int32)])[:, None]
    lane = lax.broadcasted_iota(jnp.int32, (wide, 128), 1) % HEAD_DIM
    same = group == lane
    query_side = jnp.where((lane < 5) & ~same, -BIG, 0.0).astype(BF16)
    key_side = jnp.where(same | ((lane >= 5) & (lane < 8)), 1.0, 0.0).astype(BF16)
    return query_side, key_side


def dot_nt(a, b):
    return lax.dot_general(a, b, (((1,), (1,)), ((), ())), preferred_element_type=F32)


def dot_nn(a, b):
    return lax.dot_general(a, b, (((1,), (0,)), ((), ())), preferred_element_type=F32)


def dot_tn(a, b):
    return lax.dot_general(a, b, (((0,), (0,)), ((), ())), preferred_element_type=F32)


def fill(target, value, features, keep_low, slots):
    wide = target.shape[0]
    start = slots // 16 * 16
    low_half = lax.broadcasted_iota(jnp.int32, (wide - start, 128), 1) < HEAD_DIM
    tail = features[start:wide, :] if features is not None else jnp.ones((wide - start, 128), BF16)
    target[start:wide, :] = jnp.where(low_half == keep_low, jnp.zeros_like(tail), tail)
    target[0:slots, :] = value


def forward_kernel(slots, block, q_ref, k_ref, v_ref, fq_ref, fk_ref,
                   low_ref, wide_ref, lse_ref, qa, qb, ka, kb, va, vb, out, lse):
    low_half = lax.broadcasted_iota(jnp.int32, (slots, 128), 1) < HEAD_DIM
    q = q_ref[...] * 0.125
    fq = fq_ref[0:slots, :]
    fk = fk_ref[0:slots, :]
    fill(qa, jnp.where(low_half, q, fq), fq_ref, True, slots)
    fill(qb, jnp.where(low_half, fq, q), fq_ref, False, slots)
    k = k_ref[...]
    fill(ka, jnp.where(low_half, k, fk), fk_ref, True, slots)
    fill(kb, jnp.where(low_half, fk, k), fk_ref, False, slots)
    v = v_ref[...]
    one = jnp.ones_like(v)
    fill(va, jnp.where(low_half, v, one), None, True, slots)
    fill(vb, jnp.where(low_half, one, v), None, False, slots)
    half = lax.broadcasted_iota(jnp.int32, (block, 128), 1) < HEAD_DIM

    def head(qx, kx, vx, rows):
        scores = dot_nt(qx[rows, :], kx[...])
        top = jnp.max(scores, axis=1, keepdims=True)
        weights = jnp.exp(scores - top).astype(BF16)
        return dot_nn(weights, vx[...]), top

    def step(number, carry):
        rows = pl.ds(pl.multiple_of(number * block, 16), block)
        raw_a, top_a = head(qa, ka, va, rows)
        raw_b, top_b = head(qb, kb, vb, rows)
        sums = jnp.where(half, raw_b, raw_a)
        lse[rows, :] = jnp.where(half, top_b, top_a) + jnp.log(sums)
        out[rows, :] = jnp.where(half, raw_a, raw_b) / pltpu.roll(sums, HEAD_DIM, 1)
        return carry

    lax.fori_loop(0, out.shape[0] // block, step, 0)
    attended = out[0:slots, :]
    low_ref[...] = attended.astype(BF16)
    wide_ref[...] = attended
    lse_ref[...] = lse[0:slots, :]


def column(shift, slots):
    return pl.BlockSpec((slots, 128), lambda p, s=shift: (0, s + p))


def attention_forward(qkv, fq, fk, block=240):
    slots = qkv.shape[0]
    pairs = qkv.shape[1] // 384
    wide = fq.shape[0]
    rows = round_up(slots, block)
    whole = pl.BlockSpec((wide, 128), lambda p: (0, 0))
    width = pairs * 128
    return pl.pallas_call(
        partial(forward_kernel, slots, block),
        grid=(pairs,),
        in_specs=[column(0, slots), column(pairs, slots), column(2 * pairs, slots), whole, whole],
        out_specs=[column(0, slots)] * 3,
        out_shape=[
            jax.ShapeDtypeStruct((slots, width), BF16),
            jax.ShapeDtypeStruct((slots, width), F32),
            jax.ShapeDtypeStruct((slots, width), F32),
        ],
        scratch_shapes=[pltpu.VMEM((wide, 128), BF16)] * 6 + [pltpu.VMEM((rows, 128), F32)] * 2,
        compiler_params=pltpu.CompilerParams(vmem_limit_bytes=50 * 2 ** 20),
        name="attention_forward",
    )(qkv, qkv, qkv, fq, fk)


def thirds(value):
    high = value.astype(BF16)
    rest = value - high.astype(F32)
    mid = rest.astype(BF16)
    return high, mid, (rest - mid.astype(F32)).astype(BF16)


def backward_kernel(slots, block, q_ref, k_ref, v_ref, g_ref, wide_ref, lse_ref, fq_ref, fk_ref,
                    joint_ref, sums_ref, stage, stage_sem, qa, qb, ka, kb, va, vb, ga, gb, dqa, dqb, dk, dv):
    lane = lax.broadcasted_iota(jnp.int32, (slots, 128), 1)
    low_half = lane < HEAD_DIM
    spot = lane % HEAD_DIM
    q = q_ref[...] * 0.125
    fk = fk_ref[0:slots, :]
    high, mid, low = thirds(-lse_ref[...])
    fq = jnp.where(spot == 5, high, jnp.where(spot == 6, mid, jnp.where(spot == 7, low, fq_ref[0:slots, :])))
    fill(qa, jnp.where(low_half, q, fq), fq_ref, True, slots)
    fill(qb, jnp.where(low_half, fq, q), fq_ref, False, slots)
    k = k_ref[...]
    fill(ka, jnp.where(low_half, k, fk), fk_ref, True, slots)
    fill(kb, jnp.where(low_half, fk, k), fk_ref, False, slots)
    v = v_ref[...]
    one = jnp.ones_like(v)
    fill(va, jnp.where(low_half, v, one), None, True, slots)
    fill(vb, jnp.where(low_half, one, v), None, False, slots)
    g = g_ref[...]
    product = g.astype(F32) * wide_ref[...]
    delta_a = jnp.sum(jnp.where(low_half, product, 0.0), axis=1, keepdims=True)
    delta_b = jnp.sum(jnp.where(low_half, 0.0, product), axis=1, keepdims=True)
    high, mid, low = thirds(-jnp.where(low_half, delta_b, delta_a))
    zero = jnp.zeros_like(g)
    fg = jnp.where(spot == 0, high, jnp.where(spot == 1, mid, jnp.where(spot == 2, low, zero)))
    ga[...] = jnp.zeros_like(ga)
    gb[...] = jnp.zeros_like(gb)
    ga[0:slots, :] = jnp.where(low_half, g, fg)
    gb[0:slots, :] = jnp.where(low_half, fg, g)
    dqa[...] = jnp.zeros_like(dqa)
    dqb[...] = jnp.zeros_like(dqb)
    half = lax.broadcasted_iota(jnp.int32, (block, 128), 1) < HEAD_DIM

    def head(qx, kx, vx, gx, dqx, rows):
        keys = kx[rows, :]
        probs = jnp.exp(dot_nt(keys, qx[...]))
        value_grad = dot_nn(probs.astype(BF16), gx[...])
        score_grad = (probs * dot_nt(vx[rows, :], gx[...])).astype(BF16)
        key_grad = dot_nn(score_grad, qx[...])
        dqx[...] += dot_tn(score_grad, keys)
        return key_grad, value_grad

    def step(number, carry):
        rows = pl.ds(pl.multiple_of(number * block, 16), block)
        key_a, value_a = head(qa, ka, va, ga, dqa, rows)
        key_b, value_b = head(qb, kb, vb, gb, dqb, rows)
        dk[rows, :] = jnp.where(half, key_a, key_b)
        dv[rows, :] = jnp.where(half, value_a, value_b)
        return carry

    lax.fori_loop(0, dk.shape[0] // block, step, 0)
    pair = pl.program_id(0)
    pairs = pl.num_programs(0)

    def copy_out(third, at):
        cols = pl.ds(pl.multiple_of((third * pairs + at) * 128, 128), 128)
        return pltpu.make_async_copy(stage.at[third], joint_ref.at[:, cols], stage_sem.at[third])

    query_grad = (jnp.where(low_half, dqa[0:slots, :], dqb[0:slots, :]) * 0.125).astype(BF16)
    rounded = (query_grad, dk[0:slots, :].astype(BF16), dv[0:slots, :].astype(BF16))
    for third in range(3):
        @pl.when(pair > 0)
        def _():
            copy_out(third, pair - 1).wait()

        stage[third] = rounded[third]
        copy_out(third, pair).start()
        sums_ref[0, third : third + 1, :] = jnp.sum(rounded[third].astype(F32), axis=0, keepdims=True)

    @pl.when(pair == pairs - 1)
    def _():
        for third in range(3):
            copy_out(third, pair).wait()


def attention_backward(qkv, upstream, wide_out, lse, fq, fk, block=240):
    slots = qkv.shape[0]
    pairs = qkv.shape[1] // 384
    wide = fq.shape[0]
    rows = round_up(slots, block)
    whole = pl.BlockSpec((wide, 128), lambda p: (0, 0))
    return pl.pallas_call(
        partial(backward_kernel, slots, block),
        grid=(pairs,),
        in_specs=[column(0, slots), column(pairs, slots), column(2 * pairs, slots),
                  column(0, slots), column(0, slots), column(0, slots), whole, whole],
        out_specs=[pl.BlockSpec(memory_space=pl.ANY), pl.BlockSpec((1, 8, 128), lambda p: (p, 0, 0))],
        out_shape=[jax.ShapeDtypeStruct(qkv.shape, BF16), jax.ShapeDtypeStruct((pairs, 8, 128), F32)],
        scratch_shapes=[pltpu.VMEM((3, slots, 128), BF16), pltpu.SemaphoreType.DMA((3,))]
        + [pltpu.VMEM((wide, 128), BF16)] * 8
        + [pltpu.VMEM((wide, 128), F32)] * 2 + [pltpu.VMEM((rows, 128), F32)] * 2,
        compiler_params=pltpu.CompilerParams(vmem_limit_bytes=60 * 2 ** 20),
        name="attention_backward",
    )(qkv, qkv, qkv, upstream, wide_out, lse, fq, fk)


root_half = 0.7071067811865476
inverse_root_tau = 0.3989422804014327


def expand_kernel(chunk, skip, x_ref, w_ref, b_ref, after_ref, slope_ref):
    x = x_ref[...]

    def step(number, carry):
        cols = pl.ds(pl.multiple_of(number * chunk, 128), chunk)
        weight = w_ref[:, pl.ds(pl.multiple_of(skip + number * chunk, 128), chunk)]
        before = dot_nn(x, weight) + b_ref[:, cols]
        cumulative = 0.5 * (1.0 + lax.erf(before * root_half))
        density = jnp.exp(-0.5 * before * before) * inverse_root_tau
        after_ref[:, cols] = (before * cumulative).astype(BF16)
        slope_ref[:, cols] = (cumulative + before * density).astype(BF16)
        return carry

    lax.fori_loop(0, b_ref.shape[1] // chunk, step, 0)


def expand_forward(x, weight, bias, block=240, chunk=768):
    slots, inner = x.shape
    hidden = bias.shape[0]
    skip = weight.shape[1] - hidden
    return pl.pallas_call(
        partial(expand_kernel, chunk, skip),
        grid=(round_up(slots, block) // block,),
        in_specs=[
            pl.BlockSpec((block, inner), lambda r: (r, 0)),
            pl.BlockSpec(weight.shape, lambda r: (0, 0)),
            pl.BlockSpec((1, hidden), lambda r: (0, 0)),
        ],
        out_specs=[pl.BlockSpec((block, hidden), lambda r: (r, 0))] * 2,
        out_shape=[jax.ShapeDtypeStruct((slots, hidden), BF16)] * 2,
        compiler_params=pltpu.CompilerParams(vmem_limit_bytes=40 * 2 ** 20),
        name="expand_forward",
    )(x, weight, bias.reshape(1, -1))


MESH = pl.DeviceIdType.MESH


class Place:
    def __init__(self, n_dp, n_fsdp):
        self.n_dp, self.n_fsdp, self.lines = n_dp, n_fsdp, n_fsdp // 4
        self.dp, at = lax.axis_index("dp"), lax.axis_index("fsdp")
        core = self.dp % 2
        self.stride_u, self.stride_w = 2 - core, 1 + core
        high, low = (at // 2) % 2, at % 2
        self.a = at // 4
        self.u = high * (1 - core) + low * core
        self.w = low * (1 - core) + high * core

    def fsdp_of(self, da, du, dw):
        a, u, w = (self.a + da) % self.lines, (self.u + du) % 2, (self.w + dw) % 2
        return a * 4 + u * self.stride_u + w * self.stride_w

    def dp_of(self, dd):
        return (self.dp + dd) % self.n_dp

    def piece(self, dd, da, du, dw):
        return self.dp_of(dd) * self.n_fsdp + self.fsdp_of(da, du, dw)

    def device(self, dd, da, du, dw):
        return (self.dp_of(dd), self.fsdp_of(da, du, dw))

    def slot(self, dd, da, du, dw):
        return ((dd * self.lines + da) * 2 + du) * 2 + dw

    def greet(self):
        barrier = pltpu.get_barrier_semaphore()
        friends = [(0, 0, 1, 0), (0, 0, 0, 1)]
        friends += [(0, da, 0, 0) for da in range(1, self.lines)]
        friends += [(dd, 0, 0, 0) for dd in range(1, self.n_dp)]
        for friend in friends:
            pl.semaphore_signal(barrier, inc=1, device_id=self.device(*friend), device_id_type=MESH)
        pl.semaphore_wait(barrier, len(friends))


class Sender:
    def __init__(self, place, send_sem):
        self.place, self.send_sem, self.pending = place, send_sem, []

    def prepare(self, source, target, recv_sem, device, guard=None):
        copy = pltpu.make_async_remote_copy(
            src_ref=source, dst_ref=target, send_sem=self.send_sem.at[len(self.pending)],
            recv_sem=recv_sem, device_id=self.place.device(*device), device_id_type=MESH,
        )
        self.pending.append((copy, guard))
        return copy

    def receiver(self, target, recv_sem):
        return pltpu.make_async_remote_copy(
            src_ref=target, dst_ref=target, send_sem=self.send_sem.at[0],
            recv_sem=recv_sem, device_id=self.place.device(0, 0, 0, 1), device_id_type=MESH,
        )

    def drain(self):
        for copy, guard in self.pending:
            when(guard, copy.wait_send)


def when(guard, action):
    if guard is None:
        action()
    else:
        pl.when(guard)(action)


def gather_kernel(n_dp, n_fsdp, count, *refs):
    own, full = refs[:count], refs[count : 2 * count]
    send_sem, recv_sem, local_sem = refs[2 * count :]
    place = Place(n_dp, n_fsdp)
    sender = Sender(place, send_sem)
    lines = place.lines
    here = [pltpu.make_async_copy(own[i], full[i].at[place.piece(0, 0, 0, 0)], local_sem.at[i]) for i in range(count)]
    for copy in here:
        copy.start()
    place.greet()

    def forward(piece, device, source=None, guard=None):
        dd, da, du, dw = piece
        ed, ea, eu, ew = device
        bits = ((du - eu) % 2, (dw - ew) % 2)
        seen = place.slot((dd - ed) % n_dp, (da - ea) % lines, *(bits[::-1] if ed % 2 else bits))
        copies = []
        for i in range(count):
            target = full[i].at[place.piece(*piece)]
            copies.append(sender.prepare(
                target if source is None else source[i], target, recv_sem.at[seen * count + i], device, guard
            ))
        return copies

    def awaited(piece):
        return [
            sender.receiver(full[i].at[place.piece(*piece)], recv_sem.at[place.slot(*piece) * count + i])
            for i in range(count)
        ]

    def start(copies):
        for copy in copies:
            copy.start()

    def await_piece(piece):
        for copy in awaited(piece):
            copy.wait_recv()

    spread_dp = [(dd, 0, 0, 0) for dd in range(1, n_dp)]
    last, onward, backward = (0, 0, 0, 1), (0, 1, 0, 0), (0, lines - 1, 0, 0)
    not_top, not_bottom = place.a + 1 < lines, place.a > 0

    def spread(piece, source=None):
        right = forward(piece, onward, source, not_top)
        left = forward(piece, backward, source, not_bottom)
        pl.when(not_top)(lambda: start(right))
        pl.when(not_bottom)(lambda: start(left))
        for device in [last] + spread_dp:
            start(forward(piece, device, source))

    start(forward((0, 0, 0, 0), (0, 0, 1, 0), own))
    spread((0, 0, 0, 0), own)
    await_piece((0, 0, 1, 0))
    spread((0, 0, 1, 0))

    def line_piece(distance, du, from_left):
        piece = (0, (lines - distance) if from_left else distance, du, 0)
        here_now = place.a >= distance if from_left else place.a + distance < lines
        further = here_now & (not_top if from_left else not_bottom)
        arrivals = awaited(piece)
        pass_on = forward(piece, onward if from_left else backward, None, further)
        others = [copy for device in [last] + spread_dp for copy in forward(piece, device, None, here_now)]

        def act():
            for copy in arrivals:
                copy.wait_recv()

        pl.when(here_now)(act)
        pl.when(further)(lambda: start(pass_on))
        pl.when(here_now)(lambda: start(others))

    for distance in range(1, lines):
        for du in range(2):
            for from_left in (True, False):
                line_piece(distance, du, from_left)
    for da in range(lines):
        for du in range(2):
            await_piece((0, da, du, 1))
            for device in spread_dp:
                start(forward((0, da, du, 1), device))
    for dd in range(1, n_dp):
        for da in range(lines):
            for du in range(2):
                for dw in range(2):
                    await_piece((dd, da, du, dw))
    for copy in here:
        copy.wait()
    sender.drain()


def gather_pieces(pieces, n_dp, n_fsdp, collective_id):
    count, lines, total = len(pieces), n_fsdp // 4, n_dp * n_fsdp
    line_sends = (lines - 1) * 4 * (n_dp + 1)
    sends = (1 + 2 * (n_dp + 2) + line_sends + 2 * lines * (n_dp - 1)) * count
    return pl.pallas_call(
        partial(gather_kernel, n_dp, n_fsdp, count),
        in_specs=[pl.BlockSpec(memory_space=pltpu.VMEM)] * count,
        out_specs=[pl.BlockSpec(memory_space=pltpu.VMEM)] * count,
        out_shape=[jax.ShapeDtypeStruct((total,) + piece.shape, piece.dtype) for piece in pieces],
        scratch_shapes=[
            pltpu.SemaphoreType.DMA((sends,)),
            pltpu.SemaphoreType.DMA((total * count,)),
            pltpu.SemaphoreType.DMA((count,)),
        ],
        compiler_params=pltpu.CompilerParams(
            collective_id=collective_id, has_side_effects=True, vmem_limit_bytes=40 * 2 ** 20
        ),
        name="gather_pieces",
    )(*pieces)


def scatter_kernel(n_dp, n_fsdp, count, *refs):
    parts, sums = refs[:count], refs[count : 2 * count]
    rest = refs[2 * count :]
    send_sem, recv_sem = rest[0], rest[1]
    got_dp, got_w, got_u, got_a = (rest[2 + k * count : 2 + (k + 1) * count] for k in range(4))
    put_w, put_u, put_a = (rest[2 + k * count : 2 + (k + 1) * count] for k in range(4, 7))
    place = Place(n_dp, n_fsdp)
    sender = Sender(place, send_sem)
    lines = place.lines
    base_w = (n_dp - 1) * n_fsdp
    base_u = base_w + 2 * lines
    base_a = base_u + lines
    place.greet()

    def from_dp(dd, da, du, dw):
        return (dd - 1) * n_fsdp + place.slot(0, da, du, dw)

    def send(source, target, index, base, device):
        for i in range(count):
            sender.prepare(source(i), target[i].at[index], recv_sem.at[(base + index) * count + i], device).start()

    def arrived(target, index, base):
        for i in range(count):
            sender.receiver(target[i].at[index], recv_sem.at[(base + index) * count + i]).wait_recv()

    far_first = sorted(range(1, lines), key=lambda d: -min(d, lines - d)) + [0]
    order = [(da, du, dw) for dw in (1, 0) for du in (1, 0) for da in far_first]
    for da, du, dw in order:
        for dd in range(1, n_dp):
            piece = place.piece(dd, da, *((dw, du) if dd % 2 else (du, dw)))
            send(lambda i: parts[i].at[piece], got_dp, from_dp(n_dp - dd, da, du, dw), 0, (dd, 0, 0, 0))

    def total(i, da, du, dw, extra):
        value = parts[i][place.piece(0, da, du, dw)].astype(F32)
        for dd in range(1, n_dp):
            value += got_dp[i][from_dp(dd, da, du, dw)].astype(F32)
        for ref, index in extra:
            value += ref[i][index].astype(F32)
        return value

    def await_dp(da, du, dw):
        for dd in range(1, n_dp):
            arrived(got_dp, from_dp(dd, da, du, dw), 0)

    for da, du, dw in order:
        await_dp(da, du, dw)
        if dw == 1:
            index = da * 2 + du
            for i in range(count):
                put_w[i][index] = total(i, da, du, 1, []).astype(BF16)
            send(lambda i: put_w[i].at[index], got_w, index, base_w, (0, 0, 0, 1))
    for da in far_first:
        arrived(got_w, da * 2 + 1, base_w)
        for i in range(count):
            put_u[i][da] = total(i, da, 1, 0, [(got_w, da * 2 + 1)]).astype(BF16)
        send(lambda i: put_u[i].at[da], got_u, da, base_u, (0, 0, 1, 0))
    for da in far_first:
        arrived(got_w, da * 2, base_w)
        arrived(got_u, da, base_u)
        extra = [(got_w, da * 2), (got_u, da)]
        if da:
            for i in range(count):
                put_a[i][da - 1] = total(i, da, 0, 0, extra).astype(BF16)
            send(lambda i: put_a[i].at[da - 1], got_a, lines - da - 1, base_a, (0, da, 0, 0))
    for k in range(lines - 1):
        arrived(got_a, k, base_a)
        extra.append((got_a, k))
    for i in range(count):
        sums[i][...] = total(i, 0, 0, 0, extra)
    sender.drain()


def scatter_sums(parts, n_dp, n_fsdp, collective_id):
    count, lines = len(parts), n_fsdp // 4
    copies = ((n_dp - 1) * n_fsdp + 2 * lines + lines + lines - 1) * count
    sizes = [(n_dp - 1) * n_fsdp, 2 * lines, lines, lines - 1, 2 * lines, lines, lines - 1]
    buffers = [pltpu.VMEM((size,) + part.shape[1:], BF16) for size in sizes for part in parts]
    return pl.pallas_call(
        partial(scatter_kernel, n_dp, n_fsdp, count),
        in_specs=[pl.BlockSpec(memory_space=pltpu.VMEM)] * count,
        out_specs=[pl.BlockSpec(memory_space=pltpu.VMEM)] * count,
        out_shape=[jax.ShapeDtypeStruct(part.shape[1:], F32) for part in parts],
        scratch_shapes=[pltpu.SemaphoreType.DMA((copies,)), pltpu.SemaphoreType.DMA((copies,))] + buffers,
        compiler_params=pltpu.CompilerParams(
            collective_id=collective_id, has_side_effects=True, vmem_limit_bytes=60 * 2 ** 20
        ),
        name="scatter_sums",
    )(*parts)


D = 768
FF = 3072


epsilon = 1e-06


def normalize_keep(values, gain_vector, shift_vector):
    centred = values - jnp.mean(values, axis=-1, keepdims=True)
    inverse = lax.rsqrt(jnp.mean(centred * centred, axis=-1, keepdims=True) + epsilon)
    scaled = centred * inverse
    return (scaled * gain_vector + shift_vector, scaled, inverse)


def normalize_back(upstream, scaled, inverse, gain_vector):
    weighted = upstream * gain_vector
    centred = weighted - jnp.mean(weighted, axis=-1, keepdims=True)
    result = inverse * (centred - scaled * jnp.mean(weighted * scaled, axis=-1, keepdims=True))
    return (result, jnp.sum(upstream * scaled, axis=0), jnp.sum(upstream, axis=0))


def split_vectors(small_full):
    columns = small_full.astype(jnp.float32)
    pieces = [columns[:, number] for number in range(8)]
    return (pieces, columns[:, 8:].T.reshape(FF))


def per_device(
    tokens,
    cotangent,
    segments,
    padding,
    qkv_weight,
    qkv_moment,
    qkv_average,
    merge_weight,
    merge_moment,
    merge_average,
    expand_weight,
    expand_moment,
    expand_average,
    shrink_weight,
    shrink_moment,
    shrink_average,
    small_params,
    small_moment,
    small_average,
):
    masters = (qkv_weight, merge_weight, expand_weight, shrink_weight, small_params)
    lowered = tuple((master.astype(jnp.bfloat16) for master in masters))
    low_qkv, low_merge, low_expand, low_shrink, low_small = lowered
    axes = ("dp", "fsdp")
    own_rows = qkv_weight.shape[0]
    n_dp, n_fsdp = lax.axis_size("dp"), lax.axis_size("fsdp")
    small_rows = jnp.pad(low_small.reshape(own_rows, -1), ((0, 0), (0, 128 - 8 - FF // D)))
    qkv_full, small_full = gather_pieces([low_qkv, small_rows], n_dp, n_fsdp, 0)
    qkv_full = qkv_full.reshape(D, 3 * D)
    small_full = small_full.reshape(D, 128)[:, : 8 + FF // D]
    second = jnp.concatenate([low_merge, low_expand], axis=1)
    second = lax.all_gather(second, axes, axis=0, tiled=True)
    shrink_full = lax.all_gather(low_shrink, axes, axis=0, tiled=True)
    merge_full, expand_full = second[:, :D], second[:, D:]
    pieces, bias_expand = split_vectors(small_full)
    gain_one, shift_one, bias_query, bias_value, bias_merge, gain_two, shift_two, bias_shrink = (
        pieces
    )
    inputs = tokens.astype(jnp.float32)
    query_mask, key_mask = mask_features(segments, padding, tokens.shape[0])
    norm_one, scaled_one, inverse_one = normalize_keep(inputs, gain_one, shift_one)
    norm_one_low = norm_one.astype(jnp.bfloat16)
    joined = jnp.dot(norm_one_low, qkv_full, preferred_element_type=jnp.float32)
    joined = joined + jnp.concatenate([bias_query, jnp.zeros((D,), jnp.float32), bias_value])
    joined_low = joined.astype(jnp.bfloat16)
    attended_low, attended_wide, logsums = attention_forward(joined_low, query_mask, key_mask)
    middle = (
        inputs + jnp.dot(attended_low, merge_full, preferred_element_type=jnp.float32) + bias_merge
    )
    norm_two, scaled_two, inverse_two = normalize_keep(middle, gain_two, shift_two)
    norm_two_low = norm_two.astype(jnp.bfloat16)
    after_low, slope = expand_forward(norm_two_low, second, bias_expand)
    output = (
        middle + jnp.dot(after_low, shrink_full, preferred_element_type=jnp.float32) + bias_shrink
    )
    activations = output.astype(jnp.bfloat16)
    back_gain_one, back_gain_two = gain_one, gain_two
    outgoing = cotangent.astype(jnp.float32) * padding[:, None].astype(jnp.float32)
    outgoing_low = outgoing.astype(jnp.bfloat16)
    shrink_part = jnp.einsum(
        "sf,sd->fd", after_low, outgoing_low, preferred_element_type=jnp.float32
    )
    shrink_bias_part = jnp.sum(outgoing, axis=0)
    shrink_low, shrink_full = lax.optimization_barrier((shrink_part.astype(BF16), shrink_full))
    act_grad = jnp.einsum(
        "sd,fd->sf", outgoing_low, shrink_full, preferred_element_type=jnp.float32
    )
    before_grad = (act_grad * slope.astype(F32)).astype(BF16)
    expand_part = jnp.einsum(
        "sd,sf->df", norm_two_low, before_grad, preferred_element_type=jnp.float32
    )
    expand_bias_part = jnp.sum(before_grad.astype(jnp.float32), axis=0)
    up_two = jnp.einsum("sf,df->sd", before_grad, expand_full, preferred_element_type=jnp.float32)
    second_back, gain_two_part, shift_two_part = normalize_back(
        up_two, scaled_two, inverse_two, back_gain_two
    )
    middle_grad = outgoing + second_back
    middle_low = middle_grad.astype(jnp.bfloat16)
    merge_part = jnp.einsum(
        "sd,se->de", attended_low, middle_low, preferred_element_type=jnp.float32
    )
    merge_bias_part = jnp.sum(middle_low.astype(jnp.float32), axis=0)
    attended_grad = jnp.einsum(
        "se,de->sd", middle_low, merge_full, preferred_element_type=jnp.float32
    ).astype(jnp.bfloat16)
    wide_part = jnp.concatenate([merge_part, expand_part], axis=1).astype(BF16)
    wide_part, attended_grad = lax.optimization_barrier((wide_part, attended_grad))
    qkv_grad_low, column_sums = attention_backward(
        joined_low, attended_grad, attended_wide, logsums, query_mask, key_mask
    )
    qkv_part = jnp.einsum(
        "sd,sc->dc", norm_one_low, qkv_grad_low, preferred_element_type=jnp.float32
    )
    up_one = jnp.einsum("sc,dc->sd", qkv_grad_low, qkv_full, preferred_element_type=jnp.float32)
    first_back, gain_one_part, shift_one_part = normalize_back(
        up_one, scaled_one, inverse_one, back_gain_one
    )
    input_grad = middle_grad + first_back
    vector_rows = jnp.stack(
        [
            gain_one_part,
            shift_one_part,
            column_sums[:, 0].reshape(D),
            column_sums[:, 2].reshape(D),
            merge_bias_part,
            gain_two_part,
            shift_two_part,
            shrink_bias_part,
        ]
    )
    all_rows = jnp.concatenate([vector_rows, expand_bias_part.reshape(FF // D, D)], axis=0)
    small_part = all_rows.T
    shrink_sum = lax.psum_scatter(shrink_low, axes, scatter_dimension=0, tiled=True)
    wide_sum = lax.psum_scatter(wide_part, axes, scatter_dimension=0, tiled=True).astype(F32)
    small_part = jnp.pad(small_part, ((0, 0), (0, 128 - 8 - FF // D)))
    last_parts = [part.astype(BF16).reshape(n_dp * n_fsdp, own_rows, -1) for part in (qkv_part, small_part)]
    qkv_sum, small_sum = scatter_sums(last_parts, n_dp, n_fsdp, 1)
    summed = (
        qkv_sum,
        wide_sum[:, :D],
        wide_sum[:, D:],
        shrink_sum.astype(F32),
        small_sum[:, : 8 + FF // D].reshape(-1),
    )
    rate_scale = (tokens.shape[0] * lax.axis_size("dp") * lax.axis_size("fsdp")) ** (-0.5)
    rates = (
        0.04 * rate_scale,
        4.0 * rate_scale,
        0.08 * rate_scale,
        0.02 * rate_scale,
        0.07 * rate_scale,
    )
    moments = (qkv_moment, merge_moment, expand_moment, shrink_moment, small_moment)
    averages = (qkv_average, merge_average, expand_average, shrink_average, small_average)
    results = [activations, input_grad]
    for master, gradient, moment, average, step_rate in zip(
        masters, summed, moments, averages, rates
    ):
        fresh_moment = 0.5 * moment + gradient
        updated = master - step_rate * (gradient + 0.5 * fresh_moment)
        results.extend(
            [
                gradient,
                fresh_moment,
                updated,
                0.5 * average + 0.5 * updated,
                updated.astype(jnp.bfloat16),
            ]
        )
    return tuple(results)


def solution(mesh):
    placed = (
        P(("dp", "fsdp"), None),
        P(("dp", "fsdp"), None),
        P(("dp", "fsdp")),
        P(("dp", "fsdp")),
        P(("dp", "fsdp"), None),
        P(("dp", "fsdp"), None),
        P(("dp", "fsdp"), None),
        P(("dp", "fsdp"), None),
        P(("dp", "fsdp"), None),
        P(("dp", "fsdp"), None),
        P(("dp", "fsdp"), None),
        P(("dp", "fsdp"), None),
        P(("dp", "fsdp"), None),
        P(("dp", "fsdp"), None),
        P(("dp", "fsdp"), None),
        P(("dp", "fsdp"), None),
        P(("dp", "fsdp")),
        P(("dp", "fsdp")),
        P(("dp", "fsdp")),
    )
    return jax.shard_map(
        per_device,
        mesh=mesh,
        in_specs=placed,
        out_specs=(
            P(("dp", "fsdp"), None),
            P(("dp", "fsdp"), None),
            P(("dp", "fsdp"), None),
            P(("dp", "fsdp"), None),
            P(("dp", "fsdp"), None),
            P(("dp", "fsdp"), None),
            P(("dp", "fsdp"), None),
            P(("dp", "fsdp"), None),
            P(("dp", "fsdp"), None),
            P(("dp", "fsdp"), None),
            P(("dp", "fsdp"), None),
            P(("dp", "fsdp"), None),
            P(("dp", "fsdp"), None),
            P(("dp", "fsdp"), None),
            P(("dp", "fsdp"), None),
            P(("dp", "fsdp"), None),
            P(("dp", "fsdp"), None),
            P(("dp", "fsdp"), None),
            P(("dp", "fsdp"), None),
            P(("dp", "fsdp"), None),
            P(("dp", "fsdp"), None),
            P(("dp", "fsdp"), None),
            P(("dp", "fsdp")),
            P(("dp", "fsdp")),
            P(("dp", "fsdp")),
            P(("dp", "fsdp")),
            P(("dp", "fsdp")),
        ),
        check_vma=False,
    )
```
